768 devices in a mesh: section: 48 (over x, z), row: 2 (over core), col: 8 (over y).
Axes of the slice: x: 4, y: 8, z: 12, core: 2. Of those that a mesh axis runs over, the one named last changes fastest.
Arguments:
- arriving: bfloat16 [48, 16, 16384], P('section', ('row', 'col')), may hold values from -64 to 64
- entering: bfloat16 [3, 16, 16384], P(None, ('row', 'col')), may hold values from -64 to 64
- gain: bfloat16 [48, 16384], P('section'), may hold values from 0.099609375 to 1.8984375
- kv_weight: bfloat16 [48, 16384, 1024], P('section', 'row', 'col'), may hold values from -0.046875 to 0.046875
- queries: bfloat16 [48, 4, 16, 8192], P('section', None, ('row', 'col')), may hold values from -150 to 150
- cache_keys: bfloat16 [48, 4, 16, 128, 512], P('section', None, ('row', 'col')), may hold values from -6 to 6
- cache_values: bfloat16 [48, 4, 16, 128, 512], P('section', None, ('row', 'col')), may hold values from -6 to 6
- lengths: int32 [51, 16], P(None, ('row', 'col')), may hold values from 2 to 128, as said below
Outputs:
- layer_out: bfloat16 [48, 4, 16, 16384], P('section', None, ('row', 'col'))
The draws below stay inside these ranges and needn't reach their ends.
Inputs may be any that keep to these rules, and one draw needn't show every extreme that they name: Every row of lengths has a request with exactly 128 cached tokens, at a position drawn from the seed.
All inputs are finite; a program needn't handle non-finite values.
Results may differ from the reference program's by a relative error of at most 0.0034.
Values may be sent and summed in bfloat16 or wider, within the bound.
No kernel may reach another device: no remote copies, remote signals or barrier semaphores. Data moves between devices by JAX's collectives and lax.ppermute only.
A program may use at most 32 MiB of HBM per device.

```python
import math
import jax
import jax.numpy as jnp
import numpy as np
from jax import lax

D = 16384
QH = 64
KVH = 4
HD = 128
LMAX = 128
TICKS = 4
KVW = 1024
LAYERS = 48
MB = 16
ENTRIES = 51


def shared_keys(key):
    base = jnp.clip(jax.random.normal(jax.random.fold_in(key, 101), (LAYERS, TICKS, MB, LMAX, KVH * HD), jnp.float32), -6.0, 6.0)
    return base


def draw_cache_keys(key, part):
    base = shared_keys(key)
    return base.astype(jnp.bfloat16)


def draw_queries(key, part):
    drawn = jnp.clip(jax.random.normal(jax.random.fold_in(key, 103), (LAYERS, TICKS, MB, QH * HD), jnp.float32), -6.0, 6.0)
    return drawn.astype(jnp.bfloat16)


def scaled_rows(key, salt, count):
    drawn = jnp.clip(jax.random.normal(jax.random.fold_in(key, salt), (count, MB, D), jnp.float32), -4.0, 4.0)
    low = math.log(0.4)
    high = math.log(4.0)
    row_scale = jnp.exp(jax.random.uniform(jax.random.fold_in(key, salt + 1), (count, MB, 1), jnp.float32, low, high))
    col_scale = jnp.exp(jax.random.uniform(jax.random.fold_in(key, salt + 2), (count, 1, D), jnp.float32, low, high))
    return (drawn * row_scale * col_scale).astype(jnp.bfloat16)


def draw_arriving(key, part):
    return scaled_rows(key, 201, LAYERS)


def draw_entering(key, part):
    return scaled_rows(key, 301, TICKS - 1)


def draw_lengths(key, part):
    first = jax.random.randint(jax.random.fold_in(key, 401), (ENTRIES, MB), 2, LMAX + 1)
    second = jax.random.randint(jax.random.fold_in(key, 402), (ENTRIES, MB), 2, LMAX + 1)
    longest = jax.random.randint(jax.random.fold_in(key, 403), (ENTRIES, 1), 0, MB)
    base = jnp.minimum(first, second)
    return jnp.where(jnp.arange(MB)[None, :] == longest, LMAX, base).astype(jnp.int32)


def steps_of(own_key, extent, cuts, least, top_value):
    factor_of, own = 1.0, jax.random.fold_in(own_key, 6)
    for axis_at, shards_of in cuts:
        steps = jnp.exp(jax.random.uniform(jax.random.fold_in(own, axis_at), (shards_of,), jnp.float32, least / len(cuts), top_value / len(cuts)))
        factor_of = factor_of * jnp.repeat(steps, extent[axis_at] // shards_of).reshape([-1 if axis == axis_at else 1 for axis in range(len(extent))])
    return factor_of


def gaussian(own_key, extent, scale, reach, split=(), held_as=jnp.bfloat16):
    drawn = jax.random.normal(own_key, extent, jnp.float32) * scale
    if len(split) > 0:
        drawn = steps_of(own_key, extent, split, -0.22, 0.18) * drawn
    return jnp.clip(drawn, min=-reach, max=reach).astype(held_as)


def setup_inputs(seed: int = 0) -> dict:
    key_of = jax.random.split(jax.random.key(seed), 9)
    return {
        "arriving": draw_arriving(jax.random.fold_in(key_of[8], 71), 0),
        "entering": draw_entering(jax.random.fold_in(key_of[8], 71), 0),
        "gain": jnp.clip(1.0 + 0.18 * jax.random.normal(key_of[2], (LAYERS, D), jnp.float32), 0.099609375, 1.8984375).astype(jnp.bfloat16),
        "kv_weight": gaussian(key_of[3], (LAYERS, D, KVW), D ** -0.5, 0.046875, ((0, 48), (1, 2), (2, 8))),
        "queries": draw_queries(jax.random.fold_in(key_of[8], 71), 0),
        "cache_keys": draw_cache_keys(jax.random.fold_in(key_of[8], 71), 0),
        "cache_values": gaussian(key_of[6], (LAYERS, TICKS, MB, LMAX, KVH * HD), 1.0, 6.0, ((0, 48), (2, 16))),
        "lengths": draw_lengths(jax.random.fold_in(key_of[8], 71), 0),
    }


def rotate(keys, positions):
    half = HD // 2
    steps_up = jnp.arange(half).astype(jnp.float32)
    inverse = jnp.exp(-jnp.log(jnp.float32(500000.0)) * steps_up / half)
    angle = positions.astype(jnp.float32)[:, None] * inverse[None, :]
    cosine = jnp.cos(angle)[:, None, :]
    sine = jnp.sin(angle)[:, None, :]
    first = keys[..., :half]
    second = keys[..., half:]
    return jnp.concatenate([first * cosine - second * sine, second * cosine + first * sine], axis=-1)

def layer(rows, gain_row, weight, queries, keys, values, lengths):
    count = rows.shape[0]
    wide = rows.astype(jnp.float32)
    scale = lax.rsqrt(lax.optimization_barrier(jnp.mean(wide * wide, axis=1, keepdims=True)) + 1e-05)
    normed = (wide * scale * gain_row.astype(jnp.float32)[None, :]).astype(jnp.bfloat16)
    fresh = jnp.dot(normed, weight, preferred_element_type=jnp.float32).reshape(count, KVH, 2, HD)
    new_key = rotate(fresh[:, :, 0, :], lengths).astype(jnp.bfloat16)
    new_value = fresh[:, :, 1, :].astype(jnp.bfloat16)
    factor = 1.0 / np.sqrt(HD)
    grouped = queries.reshape(count, KVH, QH // KVH, HD).astype(jnp.float32)
    cached = keys.reshape(count, LMAX, KVH, HD).astype(jnp.float32)
    stored = values.reshape(count, LMAX, KVH, HD).astype(jnp.float32)
    scores = jnp.einsum('rghd,rlgd->rghl', grouped, cached) * factor
    live = jnp.arange(LMAX)[None, :] < lengths[:, None]
    scores = jnp.where(live[:, None, None, :], scores, jnp.float32(-1e+30))
    own = jnp.einsum('rghd,rgd->rgh', grouped, new_key.astype(jnp.float32)) * factor
    top = jnp.maximum(lax.optimization_barrier(jnp.max(scores, axis=-1)), own)
    weights = jnp.exp(scores - top[..., None])
    own_weight = jnp.exp(own - top)
    total = lax.optimization_barrier(jnp.sum(weights, axis=-1)) + own_weight
    probs = (weights / total[..., None]).astype(jnp.bfloat16)
    own_prob = (own_weight / total).astype(jnp.bfloat16)
    mixed = jnp.einsum('rghl,rlgd->rghd', probs.astype(jnp.float32), stored)
    mixed = mixed + own_prob.astype(jnp.float32)[..., None] * new_value.astype(jnp.float32)[:, :, None, :]
    heads_width = QH * HD
    mixed = mixed.reshape(count, heads_width)
    joined = jnp.concatenate([wide[:, :heads_width] + mixed, wide[:, heads_width:]], axis=1)
    return joined.astype(jnp.bfloat16)

def reference(arriving, entering, gain, kv_weight, queries, cache_keys, cache_values, lengths):
    rows_now = arriving
    previous = arriving
    results = []
    for tick in range(TICKS):
        if tick > 0:
            rows_now = jnp.concatenate([entering[tick - 1][None], previous[:-1]], axis=0)
        picked = lengths[tick + LAYERS - 1 - np.arange(LAYERS)]
        previous = lax.map(lambda item: layer(*item), (rows_now, gain, kv_weight, queries[:, tick], cache_keys[:, tick], cache_values[:, tick], picked))
        results.append(previous)
    return jnp.stack(results, axis=1)
```

```python
import jax
import jax.numpy as jnp
import numpy as np
from jax import lax
from jax.sharding import PartitionSpec as P

QH = 64
KVH = 4
HD = 128
PER = QH // KVH
ALL = ("section", "row", "col")
RC = ("row", "col")
FACTOR = 1.0 / np.sqrt(HD)
bf16 = jnp.bfloat16
f32 = jnp.float32


def angles(positions):
    half = HD // 2
    steps_up = jnp.arange(half).astype(f32)
    inverse = jnp.exp(-jnp.log(f32(500000.0)) * steps_up / half)
    angle = positions.astype(f32)[:, None] * inverse[None, :]
    cosine = jnp.cos(angle)
    sine = jnp.sin(angle)
    return jnp.concatenate([cosine, cosine], 1), jnp.concatenate([-sine, sine], 1)


def cached_attention(queries, keys, values, lens):
    ticks, slots = keys.shape[:2]
    grouped = queries.reshape(ticks, KVH, PER, HD)
    cached = keys.reshape(ticks, slots, KVH, HD)
    stored = values.reshape(ticks, slots, KVH, HD)
    scores = jnp.einsum("tghd,tlgd->tghl", grouped, cached, preferred_element_type=f32)
    scores = scores * FACTOR
    live = jnp.arange(slots)[None, :] < lens[:, None]
    scores = jnp.where(live[:, None, None, :], scores, f32(-1e30))
    top = jnp.max(scores, axis=-1)
    weights = jnp.exp(scores - top[..., None])
    total = jnp.sum(weights, axis=-1)
    probs = (weights / total[..., None]).astype(bf16)
    mean = jnp.einsum("tghl,tlgd->tghd", probs, stored, preferred_element_type=f32)
    return mean, top + jnp.log(total)


def split3(x):
    hi = lax.reduce_precision(x, 8, 7)
    mid = lax.reduce_precision(x - hi, 8, 7)
    return hi, mid, (x - hi) - mid


def combine(x, mean, messages, keep):
    rows = x.shape[0]
    own = jnp.stack([messages[2 * g, :, :PER] for g in range(KVH)], 1).astype(f32)
    own = jnp.where(keep, own, 0.0)[..., None]
    new = jnp.stack([messages[2 * g + 1] for g in range(KVH)], 1).astype(f32)[:, :, None, :]
    mean = mean.reshape(rows, KVH, PER, HD).astype(f32)
    mixed = mean + own * (new - mean)
    return (x.astype(f32) + mixed.reshape(rows, QH * HD)).astype(bf16)


def project(x, gain_row, w_here, w_there, row_at, q, lse, cosine, sine, is_key):
    half = w_here.shape[0]
    wide = x.astype(f32)
    scale = lax.rsqrt(jnp.mean(wide * wide, axis=1, keepdims=True) + 1e-05)
    scaled = (wide * gain_row).astype(bf16)
    mine = lax.dynamic_slice_in_dim(scaled, row_at * half, half, 1)
    other = lax.dynamic_slice_in_dim(scaled, (1 - row_at) * half, half, 1)
    fresh = jnp.dot(mine, w_here, preferred_element_type=f32)
    fresh = fresh + jnp.dot(other, w_there, preferred_element_type=f32)
    fresh = fresh * scale
    swapped = jnp.concatenate([fresh[:, HD // 2 :], fresh[:, : HD // 2]], 1)
    key = lax.reduce_precision(fresh * cosine + swapped * sine, 8, 7)
    score = jnp.sum(q.reshape(-1, PER, HD).astype(f32) * key[:, None, :], axis=-1) * FACTOR
    own = 1.0 / (1.0 + jnp.exp(lse - score))
    own = jnp.pad(own, ((0, 0), (0, HD - PER)))
    return jnp.where(is_key, own, fresh).astype(bf16)


def per_device(arriving, entering, gain, kv_weight, queries, cache_keys, cache_values, lengths):
    section_at = lax.axis_index("section")
    row_at = lax.axis_index("row")
    col_at = lax.axis_index("col")
    sections = lax.axis_size("section")
    cols = lax.axis_size("col")
    ticks = queries.shape[1]
    width = arriving.shape[2]
    half = width // 2
    last = section_at == sections - 1
    first = section_at == 0

    def at(s, r, c):
        return ((s % sections) * 2 + r) * cols + c

    def links(pairs):
        return [(at(s, r, c), at(v, w, c)) for s, r, v, w in pairs for c in range(cols)]

    def relay_group(r):
        return [
            [at(s, r, c) for c in range(cols)] + [at(s + 1, 1 - r, c) for c in range(cols)]
            for s in range(sections)
        ]

    w_here = kv_weight[0]
    w_there = lax.ppermute(w_here, "row", [(0, 1), (1, 0)])
    gain_row = gain[0].astype(f32)[None, :]
    lens = lax.dynamic_slice_in_dim(lengths[:, 0], sections - 1 - section_at, ticks, 0)
    mean, lse = cached_attention(queries[0, :, 0], cache_keys[0, :, 0], cache_values[0, :, 0], lens)

    flat = mean.reshape(ticks, half).astype(bf16)
    fed = jnp.where(last, entering[:, 0, :half], flat[: ticks - 1])
    tail = jnp.where(first, entering[0, 0, half:], jnp.where(last, entering[1, 0, half:], entering[2, 0, half:]))
    parts = jnp.stack(split3(lse), 1).astype(bf16)
    asked = queries[0, :, 0].reshape(ticks, KVH, PER * HD)

    def block(body, slots):
        per_group = []
        for g in range(KVH):
            aux = [jnp.stack([lens[t] for t in slots]).astype(bf16), jnp.zeros((14,), bf16)]
            aux += [parts[t, :, g].reshape(-1) for t in slots]
            aux = jnp.concatenate(aux)
            aux = jnp.pad(aux, (0, 8 * HD - aux.shape[0]))
            one = jnp.concatenate([*body, *[asked[t, g] for t in slots], aux])
            per_group += [one, one]
        return per_group

    sent = block([arriving[0, 0], fed[1]], (0, 2)) + block([fed[2], tail, fed[0]], (1, 3))
    sent = jnp.stack(sent).reshape(2 * cols, -1, HD)
    got = lax.all_to_all(sent, RC, split_axis=0, concat_axis=0, tiled=True)
    got = got.reshape(2 * cols, -1)

    around = range(sections)
    mean_a = lax.ppermute(got[:, width : width + half], ALL, links([(s, r, s + 1, r) for s in around for r in (0, 1)]))
    mean_b = lax.ppermute(got[:, :half], ALL, links([(s, 1, s + 1, 1) for s in around]))
    tails = lax.ppermute(got[:, half:width], ALL, links([(sections - 1, 1, 0, 0), (1, 1, 0, 1)]))
    q_at = width + half
    aux_at = q_at + 2 * PER * HD
    asks, lses, turns = [], [], []
    for k in range(2):
        asks.append(got[:, q_at + k * PER * HD : q_at + (k + 1) * PER * HD])
        three = got[:, aux_at + 16 + 48 * k : aux_at + 64 + 48 * k].astype(f32)
        lses.append(three[:, :16] + three[:, 16:32] + three[:, 32:])
        turns.append(angles(got[:, aux_at + k].astype(f32)))
    is_key = col_at % 2 == 0

    x = got[:, :width]
    rows, messages = [], []
    for tick in range(ticks):
        if tick > 0:
            there = (tick - 1) % 2
            relayed = lax.ppermute(x, ALL, links([(s, there, s + 1, 1 - there) for s in range(sections - 1)]))
            send = jnp.broadcast_to(message[None], (2 * cols, *message.shape))
            heard = lax.all_to_all(send, ALL, split_axis=0, concat_axis=0, axis_index_groups=relay_group(there), tiled=True)
            head = combine(relayed[:, :half], mean_b if tick == 3 else mean_a, heard[:cols], jnp.logical_not(first))
            rest = jnp.where(first, got[:, half:width] if tick == 1 else tails, relayed[:, half:])
            x = jnp.concatenate([head, rest], axis=1)
        k = tick // 2
        message = project(x, gain_row, w_here, w_there, row_at, asks[k], lses[k], *turns[k], is_key)
        rows.append(x)
        messages.append(message)

    mine, other, told = [], [], []
    for k in range(2):
        for keep, r in ((mine, row_at), (other, 1 - row_at)):
            a = lax.dynamic_slice_in_dim(rows[2 * k], r * cols + col_at, 1, 0)
            b = lax.dynamic_slice_in_dim(rows[2 * k + 1], r * cols + col_at, 1, 0)
            keep.append(jnp.where(row_at == 0, a, b))
        told.append(jnp.where(row_at == 0, messages[2 * k], messages[2 * k + 1]))
    swapped = lax.ppermute(jnp.concatenate(other, 0), "row", [(0, 1), (1, 0)])
    told = lax.all_to_all(jnp.stack(told, 1), RC, split_axis=0, concat_axis=0, tiled=True)
    outputs = []
    for tick in range(ticks):
        k, r = tick // 2, tick % 2
        row = jnp.where(row_at == r, mine[k], swapped[k : k + 1])
        heard = told[r * cols : (r + 1) * cols, k][:, None, :]
        head = combine(row[:, :half], mean[tick].reshape(1, half), heard, True)
        outputs.append(jnp.concatenate([head, row[:, half:]], axis=1))
    return jnp.stack(outputs, axis=0)[None]


def solution(mesh):
    placed = (
        P("section", ("row", "col"), None),
        P(None, ("row", "col"), None),
        P("section", None),
        P("section", "row", "col"),
        P("section", None, ("row", "col"), None),
        P("section", None, ("row", "col"), None, None),
        P("section", None, ("row", "col"), None, None),
        P(None, ("row", "col")),
    )
    return jax.shard_map(
        per_device,
        mesh=mesh,
        in_specs=placed,
        out_specs=P("section", None, ("row", "col"), None),
        check_vma=False,
    )
```

```python
import functools

import jax
import jax.numpy as jnp
import numpy as np
from jax import lax
from jax.experimental import pallas as pl
from jax.experimental.pallas import tpu as pltpu
from jax.sharding import PartitionSpec as P

QH = 64
KVH = 4
HD = 128
PER = QH // KVH
ALL = ("section", "row", "col")
RC = ("row", "col")
FACTOR = 1.0 / np.sqrt(HD)
bf16 = jnp.bfloat16
f32 = jnp.float32


def angles(positions):
    half = HD // 2
    steps_up = jnp.arange(half).astype(f32)
    inverse = jnp.exp(-jnp.log(f32(500000.0)) * steps_up / half)
    angle = positions.astype(f32)[:, None] * inverse[None, :]
    cosine = jnp.cos(angle)
    sine = jnp.sin(angle)
    return jnp.concatenate([cosine, cosine], 1), jnp.concatenate([-sine, sine], 1)


def attend(qs, k_ref, v_ref, lens, scores, ticks):
    for i, t in enumerate(ticks):
        for g in range(KVH):
            q = qs[t * QH + g * PER : t * QH + (g + 1) * PER, :].astype(bf16)
            k = k_ref[i, :, g * HD : (g + 1) * HD]
            scores[i * QH + g * PER : i * QH + (g + 1) * PER, :] = lax.dot_general(
                q, k, (((1,), (1,)), ((), ())), preferred_element_type=f32
            )
    means, lses = [], []
    lane = lax.broadcasted_iota(jnp.int32, (QH, HD), 1)
    for i, t in enumerate(ticks):
        part = scores[i * QH : (i + 1) * QH, :] * FACTOR
        part = jnp.where(lane < lens[t], part, f32(-1e30))
        top = jnp.max(part, axis=1, keepdims=True)
        weights = jnp.exp(part - top)
        total = jnp.sum(weights, axis=1, keepdims=True)
        probs = (weights / total).astype(bf16)
        lses.append(top + jnp.log(total))
        for g in range(KVH):
            v = v_ref[i, :, g * HD : (g + 1) * HD]
            means.append(jnp.dot(probs[g * PER : (g + 1) * PER], v, preferred_element_type=f32))
    return means, lses


def spread(lse, tick):
    hi = lse.astype(bf16).astype(f32)
    mid = (lse - hi).astype(bf16).astype(f32)
    low = (lse - hi) - mid
    lane = lax.broadcasted_iota(jnp.int32, (PER, HD), 1)
    row = lax.broadcasted_iota(jnp.int32, (PER, HD), 0)
    out = []
    for g in range(KVH):
        total = jnp.zeros((PER, HD), f32)
        for p, part in enumerate((hi, mid, low)):
            there = lane == row + (16 + 48 * (tick // 2) + 16 * p)
            total = total + jnp.where(there, part[g * PER : (g + 1) * PER], 0.0)
        out.append(jnp.sum(total, axis=0, keepdims=True))
    return out


def first_kernel(lens, q_ref, k_ref, v_ref, mean_ref, fed_ref, aux_ref, qs, scores):
    for h in range(QH):
        qs[pl.ds(h, 4, stride=QH), :] = q_ref[:, h * HD : (h + 1) * HD].astype(f32)
    means, lses = attend(qs, k_ref, v_ref, lens, scores, (0, 1, 2))
    for n, mean in enumerate(means):
        mean_ref[n * PER : (n + 1) * PER, :] = mean
        fed_ref[n * PER : (n + 1) * PER, :] = mean.astype(bf16)
    even, odd, late = (spread(lses[t], t) for t in (0, 1, 2))
    for g in range(KVH):
        aux_ref[g : g + 1, :] = even[g] + late[g]
        aux_ref[KVH + g : KVH + g + 1, :] = odd[g]


def second_kernel(lens, pick, q_ref, k_ref, v_ref, row_ref, ent_ref, aux_in, mean_ref, own_ref, tail_ref, head_ref, ask_ref, aux_ref, qs, scores, wide, ents):
    blocks = 2 * QH
    for h in range(QH):
        qs[pl.ds(h, 4, stride=QH), :] = q_ref[:, h * HD : (h + 1) * HD].astype(f32)
    for a in range(blocks):
        wide[a : a + 1, :] = row_ref[:, a * HD : (a + 1) * HD].astype(f32)
        ents[pl.ds(a, 3, stride=blocks), :] = ent_ref[:, a * HD : (a + 1) * HD].astype(f32)
    ask_ref[...] = qs[...].astype(bf16)
    own_ref[...] = wide[...].astype(bf16)
    chosen = pl.multiple_of(pick[0] * blocks + QH, QH)
    tail_ref[...] = ents[pl.ds(chosen, QH), :].astype(bf16)
    for t in range(3):
        head_ref[t * QH : (t + 1) * QH, :] = ents[t * blocks : t * blocks + QH, :].astype(bf16)
    means, lses = attend(qs, k_ref, v_ref, lens, scores, (3,))
    for n, mean in enumerate(means):
        mean_ref[n * PER : (n + 1) * PER, :] = mean
    late = spread(lses[0], 3)
    lane = lax.broadcasted_iota(jnp.int32, (1, HD), 1)
    for r in range(2):
        known = jnp.where(lane == 0, lens[r].astype(f32), 0.0)
        known = known + jnp.where(lane == 1, lens[2 + r].astype(f32), 0.0)
        for g in range(KVH):
            n = r * KVH + g
            row = aux_in[n : n + 1, :] + known
            aux_ref[n : n + 1, :] = row + late[g] if r else row


def third_kernel(flags, fed_ref, head_ref, own_ref, tail_ref, ask_ref, aux_ref, send_ref):
    first = jnp.full((3 * QH, HD), flags[0], jnp.int32) > 0
    fed = jnp.where(first, head_ref[...].astype(f32), fed_ref[...].astype(f32)).astype(bf16)
    own = own_ref[...]
    tail = tail_ref[...]
    pad = jnp.zeros((8, HD), f32)
    sub = lax.broadcasted_iota(jnp.int32, (8, HD), 0)
    for g in range(KVH):
        for r in range(2):
            aux = jnp.where(sub == 0, jnp.broadcast_to(aux_ref[r * KVH + g : r * KVH + g + 1, :], (8, HD)), pad)
            asks = [ask_ref[t * QH + g * PER : t * QH + (g + 1) * PER, :] for t in (r, 2 + r)]
            for c in (2 * g, 2 * g + 1):
                d = 8 * r + c
                if r == 0:
                    send_ref[d, : 2 * QH, :] = own
                    send_ref[d, 2 * QH : 3 * QH, :] = fed[QH : 2 * QH]
                else:
                    send_ref[d, :QH, :] = fed[2 * QH :]
                    send_ref[d, QH : 2 * QH, :] = tail
                    send_ref[d, 2 * QH : 3 * QH, :] = fed[:QH]
                send_ref[d, 3 * QH : 3 * QH + PER, :] = asks[0]
                send_ref[d, 3 * QH + PER : 3 * QH + 2 * PER, :] = asks[1]
                send_ref[d, 3 * QH + 2 * PER :, :] = aux.astype(bf16)


def prepare(queries, keys, values, row, entering, lens, pick, first, shift):
    slots, kept = keys.shape[1], KVH * HD
    held = pl.BlockSpec(memory_space=pltpu.VMEM)
    small = pl.BlockSpec(memory_space=pltpu.SMEM)

    def cost(n):
        return pl.CostEstimate(flops=n, bytes_accessed=n, transcendentals=0)

    mean, fed, aux = pl.pallas_call(
        first_kernel,
        grid=(1,),
        out_shape=(
            jax.ShapeDtypeStruct((3 * QH, HD), f32),
            jax.ShapeDtypeStruct((3 * QH, HD), bf16),
            jax.ShapeDtypeStruct((2 * KVH, HD), f32),
        ),
        in_specs=[small, held, *[pl.BlockSpec((3, slots, kept), lambda i: (0, 0, 0))] * 2],
        out_specs=(held, held, held),
        scratch_shapes=[pltpu.VMEM((4 * QH, HD), f32), pltpu.VMEM((3 * QH, slots), f32)],
        cost_estimate=cost(4 << 20),
        compiler_params=pltpu.CompilerParams(vmem_limit_bytes=8 << 20),
        name="first_part",
    )(lens, queries, keys, values)
    fed = shift(fed)
    late, own, tail, head, ask, aux = pl.pallas_call(
        second_kernel,
        grid=(1,),
        out_shape=(
            jax.ShapeDtypeStruct((QH, HD), f32),
            jax.ShapeDtypeStruct((2 * QH, HD), bf16),
            jax.ShapeDtypeStruct((QH, HD), bf16),
            jax.ShapeDtypeStruct((3 * QH, HD), bf16),
            jax.ShapeDtypeStruct((4 * QH, HD), bf16),
            jax.ShapeDtypeStruct((2 * KVH, HD), f32),
        ),
        in_specs=[small, small, held, *[pl.BlockSpec((1, slots, kept), lambda i: (3, 0, 0))] * 2, held, held, held],
        out_specs=(held,) * 6,
        scratch_shapes=[
            pltpu.VMEM((4 * QH, HD), f32),
            pltpu.VMEM((QH, slots), f32),
            pltpu.VMEM((2 * QH, HD), f32),
            pltpu.VMEM((6 * QH, HD), f32),
        ],
        cost_estimate=cost(16 << 20),
        compiler_params=pltpu.CompilerParams(vmem_limit_bytes=8 << 20),
        name="second_part",
    )(lens, pick, queries, keys, values, row, entering, aux)
    sent = pl.pallas_call(
        third_kernel,
        out_shape=jax.ShapeDtypeStruct((16, 3 * QH + 2 * PER + 8, HD), bf16),
        in_specs=[small, held, held, held, held, held, held],
        out_specs=held,
        cost_estimate=cost(1 << 20),
        compiler_params=pltpu.CompilerParams(vmem_limit_bytes=8 << 20),
        name="third_part",
    )(first, fed, head, own, tail, ask, aux)
    return sent, mean, late


def tick_kernel(tick, *refs):
    combined = tick > 0
    flags, a_ref, b_ref, ask_ref, aux_ref, turn_ref, gain_ref, here_ref, there_ref = refs[:9]
    refs = refs[9:]
    if combined:
        heard_ref, mean_ref, extra_ref = refs[:3]
        refs = refs[3:]
    x_ref, message_ref, scaled = refs
    half = QH * HD
    rows = x_ref.shape[0]
    first = jnp.full((rows, HD), flags[2], jnp.int32) > 0
    lane = lax.broadcasted_iota(jnp.int32, (rows, HD), 1)
    square = jnp.zeros((rows, HD), f32)
    for n in range(2 * QH):
        h = n % QH
        at = slice(h * HD, (h + 1) * HD)
        if n < QH:
            x = a_ref[:, at]
            if combined:
                if h % PER == 0:
                    g = h // PER
                    own = jnp.where(first, 0.0, heard_ref[2 * g].astype(f32))
                    new = heard_ref[2 * g + 1].astype(f32)
                mean = mean_ref[:, at].astype(f32)
                weight = own[:, h % PER : h % PER + 1]
                x = (x.astype(f32) + (mean + weight * (new - mean))).astype(bf16)
        else:
            x = b_ref[:, at]
            if combined:
                x = jnp.where(first, extra_ref[:, at].astype(f32), x.astype(f32)).astype(bf16)
        x_ref[:, n * HD : (n + 1) * HD] = x
        wide = x.astype(f32)
        square = square + wide * wide
        scaled[n // QH, :, at] = (wide * gain_ref[:, n * HD : (n + 1) * HD].astype(f32)).astype(bf16)
    fresh = jnp.zeros((rows, HD), f32)
    step = 2048
    for ref, part in ((here_ref, flags[0]), (there_ref, 1 - flags[0])):
        for k in range(0, half, step):
            fresh = fresh + jnp.dot(scaled[part, :, k : k + step], ref[k : k + step, :], preferred_element_type=f32)
    scale = lax.rsqrt(jnp.sum(square, axis=1, keepdims=True) / (2 * half) + 1e-05)
    fresh = fresh * scale
    key = fresh * turn_ref[0] + pltpu.roll(fresh, HD // 2, 1) * turn_ref[1]
    key = key.astype(bf16).astype(f32)
    score = jnp.zeros((rows, HD), f32)
    for i in range(PER):
        one = jnp.sum(ask_ref[:, i * HD : (i + 1) * HD].astype(f32) * key, axis=1, keepdims=True)
        score = jnp.where(lane == i, one, score)
    aux = aux_ref[:, :HD].astype(f32)
    lse = jnp.zeros((rows, HD), f32)
    for p in range(3):
        lse = lse + pltpu.roll(aux, HD - (16 + 48 * (tick // 2) + 16 * p), 1)
    own = jnp.where(lane < PER, 1.0 / (1.0 + jnp.exp(lse - score * FACTOR)), 0.0)
    is_key = jnp.full((rows, HD), flags[1], jnp.int32) > 0
    message = jnp.where(is_key, own, fresh).astype(bf16)
    for d in range(message_ref.shape[0]):
        message_ref[d] = message


def do_tick(tick, flags, x, got, turn, gain, here, there, heard=None, extra=None):
    rows, half = got.shape[0], QH * HD
    small = pl.BlockSpec(memory_space=pltpu.SMEM)
    held = pl.BlockSpec(memory_space=pltpu.VMEM)

    def block(size, n):
        return pl.BlockSpec((rows, size), lambda i: (0, n))

    k = tick // 2
    specs = [small, block(half, 0), block(half, 1), block(PER * HD, 12 + k), block(8 * HD, 28), held, held, held, held]
    operands = [flags, x, x, got, got, turn, gain, here, there]
    if tick:
        specs += [held, block(half, 0 if tick == 3 else 2), held if tick > 1 else block(half, 1)]
        operands += [heard, got, extra]
    return pl.pallas_call(
        functools.partial(tick_kernel, tick),
        grid=(1,),
        out_shape=(
            jax.ShapeDtypeStruct((rows, 2 * half), bf16),
            jax.ShapeDtypeStruct((rows, rows, HD), bf16),
        ),
        in_specs=specs,
        out_specs=(held, held),
        scratch_shapes=[pltpu.VMEM((2, rows, half), bf16)],
        cost_estimate=pl.CostEstimate(flops=1 << 26, bytes_accessed=6 << 20, transcendentals=0),
        compiler_params=pltpu.CompilerParams(vmem_limit_bytes=20 << 20),
        name=f"tick_{tick}",
    )(*operands)


def pick_kernel(flags, a_ref, b_ref, mine_ref, other_ref):
    rows, width = a_ref.shape
    sub = lax.broadcasted_iota(jnp.int32, (8, rows), 0)
    lane = lax.broadcasted_iota(jnp.int32, (8, rows), 1)
    wanted = jnp.where(sub == 0, flags[0] * 8 + flags[3], (1 - flags[0]) * 8 + flags[3])
    select = jnp.where((lane == wanted) & (sub < 2), 1.0, 0.0).astype(bf16)
    for r, ref in enumerate((a_ref, b_ref)):

        @pl.when(flags[0] == r)
        def _():
            for k in range(0, width, 2048):
                both = jnp.dot(select, ref[:, k : k + 2048], preferred_element_type=f32)
                mine_ref[:, k : k + 2048] = both[0:1].astype(bf16)
                other_ref[:, k : k + 2048] = both[1:2].astype(bf16)


def pick_rows(flags, a, b):
    held = pl.BlockSpec(memory_space=pltpu.VMEM)
    row = jax.ShapeDtypeStruct((1, a.shape[1]), bf16)
    return pl.pallas_call(
        pick_kernel,
        out_shape=(row, row),
        in_specs=[pl.BlockSpec(memory_space=pltpu.SMEM), held, held],
        out_specs=(held, held),
        cost_estimate=pl.CostEstimate(flops=1 << 20, bytes_accessed=2 << 20, transcendentals=0),
        compiler_params=pltpu.CompilerParams(vmem_limit_bytes=8 << 20),
        name="pick_rows",
    )(flags, a, b)


def last_kernel(row_ref, told_ref, early_ref, late_ref, out_ref, tell, mean):
    half = QH * HD
    mean[: 3 * QH, :] = early_ref[...]
    mean[3 * QH :, :] = late_ref[...]
    for c in range(8):
        for r in range(2):
            for k in range(2):
                t = 2 * k + r
                tell[c, t : t + 1, :] = told_ref[8 * r + c, k : k + 1, :].astype(f32)
    for h in range(QH):
        g, i = h // PER, h % PER
        at = slice(h * HD, (h + 1) * HD)
        cached = mean[pl.ds(h, 4, stride=QH), :]
        own = tell[2 * g][:, i : i + 1]
        mixed = cached + own * (tell[2 * g + 1] - cached)
        out_ref[:, at] = (row_ref[:, at].astype(f32) + mixed).astype(bf16)
    out_ref[:, half:] = row_ref[:, half:]


def finish(row, told, early, late):
    held = pl.BlockSpec(memory_space=pltpu.VMEM)
    return pl.pallas_call(
        last_kernel,
        out_shape=jax.ShapeDtypeStruct(row.shape, bf16),
        in_specs=[held] * 4,
        out_specs=held,
        scratch_shapes=[pltpu.VMEM((8, 4, HD), f32), pltpu.VMEM((4 * QH, HD), f32)],
        cost_estimate=pl.CostEstimate(flops=1 << 20, bytes_accessed=1 << 20, transcendentals=0),
        compiler_params=pltpu.CompilerParams(vmem_limit_bytes=8 << 20),
        name="last_part",
    )(row, told, early, late)


def per_device(arriving, entering, gain, kv_weight, queries, cache_keys, cache_values, lengths):
    section_at = lax.axis_index("section")
    row_at = lax.axis_index("row")
    col_at = lax.axis_index("col")
    sections = lax.axis_size("section")
    cols = lax.axis_size("col")
    ticks = queries.shape[1]
    width = arriving.shape[2]
    half = width // 2
    last = section_at == sections - 1
    first = section_at == 0

    def at(s, r, c):
        return ((s % sections) * 2 + r) * cols + c

    def links(pairs):
        return [(at(s, r, c), at(v, w, c)) for s, r, v, w in pairs for c in range(cols)]

    def relay_group(r):
        return [
            [at(s, r, c) for c in range(cols)] + [at(s + 1, 1 - r, c) for c in range(cols)]
            for s in range(sections)
        ]

    w_here = kv_weight[0]
    w_there = lax.ppermute(w_here, "row", [(0, 1), (1, 0)])
    lens = lax.dynamic_slice_in_dim(lengths[:, 0], sections - 1 - section_at, ticks, 0)
    pick = jnp.where(first, 0, jnp.where(last, 1, 2)).astype(jnp.int32)[None]
    sent, early, late = prepare(
        queries[0, :, 0],
        cache_keys[0, :, 0],
        cache_values[0, :, 0],
        arriving[0],
        entering[:, 0],
        lens,
        pick,
        first.astype(jnp.int32)[None],
        lambda fed: lax.ppermute(fed, "section", [(s, s + 1) for s in range(sections - 1)]),
    )
    got = lax.all_to_all(sent, RC, split_axis=0, concat_axis=0, tiled=True)
    got = got.reshape(2 * cols, -1)

    tails = lax.ppermute(got[:, half:width], ALL, links([(sections - 1, 1, 0, 0), (1, 1, 0, 1)]))
    aux_at = width + half + 2 * PER * HD
    turns = [jnp.stack(angles(got[:, aux_at + k].astype(f32))) for k in range(2)]
    flags = jnp.stack([row_at, 1 - col_at % 2, first.astype(jnp.int32), col_at]).astype(jnp.int32)

    rows, messages = [], []
    for tick in range(ticks):
        step = functools.partial(do_tick, tick, flags, got=got, turn=turns[tick // 2], gain=gain, here=w_here, there=w_there)
        if tick == 0:
            x, message = step(got)
        else:
            there = (tick - 1) % 2
            relayed = lax.ppermute(x, ALL, links([(s, there, s + 1, 1 - there) for s in range(sections - 1)]))
            heard = lax.all_to_all(message, ALL, split_axis=0, concat_axis=0, axis_index_groups=relay_group(there), tiled=True)
            x, message = step(relayed, heard=heard, extra=got if tick == 1 else tails)
        rows.append(x)
        messages.append(message[0])

    told, mine, swapped = [], [], []
    for k in range(2):
        here, other = pick_rows(flags, rows[2 * k], rows[2 * k + 1])
        mine.append(here)
        swapped.append(lax.ppermute(other, "row", [(0, 1), (1, 0)]))
        told.append(jnp.where(row_at == 0, messages[2 * k], messages[2 * k + 1]))
    told = lax.all_to_all(jnp.stack(told, 1), RC, split_axis=0, concat_axis=0, tiled=True)
    pairs = [[jnp.where(row_at == r, mine[k], swapped[k]) for r in range(2)] for k in range(2)]
    out = finish(jnp.concatenate(pairs[0] + pairs[1], 0), told, early, late)
    return out[None, :, None]


def solution(mesh):
    placed = (
        P("section", ("row", "col"), None),
        P(None, ("row", "col"), None),
        P("section", None),
        P("section", "row", "col"),
        P("section", None, ("row", "col"), None),
        P("section", None, ("row", "col"), None, None),
        P("section", None, ("row", "col"), None, None),
        P(None, ("row", "col")),
    )
    return jax.shard_map(
        per_device,
        mesh=mesh,
        in_specs=placed,
        out_specs=P("section", None, ("row", "col"), None),
        check_vma=False,
    )
```

```python
import functools

import jax
import jax.numpy as jnp
import numpy as np
from jax import lax
from jax.experimental import pallas as pl
from jax.experimental.pallas import tpu as pltpu
from jax.sharding import PartitionSpec as P


QH = 64
KVH = 4
HD = 128
PER = QH // KVH
ALL = ("section", "row", "col")
RC = ("row", "col")
FACTOR = 1.0 / np.sqrt(HD)
bf16 = jnp.bfloat16
f32 = jnp.float32


def angles(positions):
    half = HD // 2
    steps_up = jnp.arange(half).astype(f32)
    inverse = jnp.exp(-jnp.log(f32(500000.0)) * steps_up / half)
    angle = positions.astype(f32)[:, None] * inverse[None, :]
    cosine = jnp.cos(angle)
    sine = jnp.sin(angle)
    return jnp.concatenate([cosine, cosine], 1), jnp.concatenate([-sine, sine], 1)


def attend(qs, k_ref, v_ref, lens, scores, ticks):
    for i, t in enumerate(ticks):
        for g in range(KVH):
            q = qs[t * QH + g * PER : t * QH + (g + 1) * PER, :].astype(bf16)
            k = k_ref[i, :, g * HD : (g + 1) * HD]
            scores[i * QH + g * PER : i * QH + (g + 1) * PER, :] = lax.dot_general(
                q, k, (((1,), (1,)), ((), ())), preferred_element_type=f32
            )
    means, lses = [], []
    lane = lax.broadcasted_iota(jnp.int32, (QH, HD), 1)
    for i, t in enumerate(ticks):
        part = scores[i * QH : (i + 1) * QH, :] * FACTOR
        part = jnp.where(lane < lens[t], part, f32(-1e30))
        top = jnp.max(part, axis=1, keepdims=True)
        weights = jnp.exp(part - top)
        total = jnp.sum(weights, axis=1, keepdims=True)
        probs = (weights / total).astype(bf16)
        lses.append(top + jnp.log(total))
        for g in range(KVH):
            v = v_ref[i, :, g * HD : (g + 1) * HD]
            means.append(jnp.dot(probs[g * PER : (g + 1) * PER], v, preferred_element_type=f32))
    return means, lses


def spread(lse, tick):
    hi = lse.astype(bf16).astype(f32)
    mid = (lse - hi).astype(bf16).astype(f32)
    low = (lse - hi) - mid
    lane = lax.broadcasted_iota(jnp.int32, (PER, HD), 1)
    row = lax.broadcasted_iota(jnp.int32, (PER, HD), 0)
    out = []
    for g in range(KVH):
        total = jnp.zeros((PER, HD), f32)
        for p, part in enumerate((hi, mid, low)):
            there = lane == row + (16 + 48 * (tick // 2) + 16 * p)
            total = total + jnp.where(there, part[g * PER : (g + 1) * PER], 0.0)
        out.append(jnp.sum(total, axis=0, keepdims=True))
    return out


def first_kernel(lens, q_ref, k_ref, v_ref, mean_ref, fed_ref, aux_ref, qs, scores):
    for h in range(QH):
        qs[pl.ds(h, 4, stride=QH), :] = q_ref[:, h * HD : (h + 1) * HD].astype(f32)
    means, lses = attend(qs, k_ref, v_ref, lens, scores, (0, 1, 2))
    for n, mean in enumerate(means):
        mean_ref[n * PER : (n + 1) * PER, :] = mean
        fed_ref[n * PER : (n + 1) * PER, :] = mean.astype(bf16)
    even, odd, late = (spread(lses[t], t) for t in (0, 1, 2))
    for g in range(KVH):
        aux_ref[g : g + 1, :] = even[g] + late[g]
        aux_ref[KVH + g : KVH + g + 1, :] = odd[g]


def second_kernel(lens, pick, q_ref, k_ref, v_ref, row_ref, ent_ref, aux_in, mean_ref, own_ref, tail_ref, head_ref, ask_ref, aux_ref, qs, scores, wide, ents):
    blocks = 2 * QH
    for h in range(QH):
        qs[pl.ds(h, 4, stride=QH), :] = q_ref[:, h * HD : (h + 1) * HD].astype(f32)
    for a in range(blocks):
        wide[a : a + 1, :] = row_ref[:, a * HD : (a + 1) * HD].astype(f32)
        ents[pl.ds(a, 3, stride=blocks), :] = ent_ref[:, a * HD : (a + 1) * HD].astype(f32)
    ask_ref[...] = qs[...].astype(bf16)
    own_ref[...] = wide[...].astype(bf16)
    chosen = pl.multiple_of(pick[0] * blocks + QH, QH)
    tail_ref[...] = ents[pl.ds(chosen, QH), :].astype(bf16)
    for t in range(3):
        head_ref[t * QH : (t + 1) * QH, :] = ents[t * blocks : t * blocks + QH, :].astype(bf16)
    means, lses = attend(qs, k_ref, v_ref, lens, scores, (3,))
    for n, mean in enumerate(means):
        mean_ref[n * PER : (n + 1) * PER, :] = mean
    late = spread(lses[0], 3)
    lane = lax.broadcasted_iota(jnp.int32, (1, HD), 1)
    for r in range(2):
        known = jnp.where(lane == 0, lens[r].astype(f32), 0.0)
        known = known + jnp.where(lane == 1, lens[2 + r].astype(f32), 0.0)
        for g in range(KVH):
            n = r * KVH + g
            row = aux_in[n : n + 1, :] + known
            aux_ref[n : n + 1, :] = row + late[g] if r else row


def third_kernel(flags, fed_ref, head_ref, own_ref, tail_ref, ask_ref, aux_ref, send_ref):
    first = jnp.full((3 * QH, HD), flags[0], jnp.int32) > 0
    fed = jnp.where(first, head_ref[...].astype(f32), fed_ref[...].astype(f32)).astype(bf16)
    own = own_ref[...]
    tail = tail_ref[...]
    pad = jnp.zeros((8, HD), f32)
    sub = lax.broadcasted_iota(jnp.int32, (8, HD), 0)
    for g in range(KVH):
        for r in range(2):
            aux = jnp.where(sub == 0, jnp.broadcast_to(aux_ref[r * KVH + g : r * KVH + g + 1, :], (8, HD)), pad)
            asks = [ask_ref[t * QH + g * PER : t * QH + (g + 1) * PER, :] for t in (r, 2 + r)]
            for c in (2 * g, 2 * g + 1):
                d = 8 * r + c
                if r == 0:
                    send_ref[d, : 2 * QH, :] = own
                    send_ref[d, 2 * QH : 3 * QH, :] = fed[QH : 2 * QH]
                else:
                    send_ref[d, :QH, :] = fed[2 * QH :]
                    send_ref[d, QH : 2 * QH, :] = tail
                    send_ref[d, 2 * QH : 3 * QH, :] = fed[:QH]
                send_ref[d, 3 * QH : 3 * QH + PER, :] = asks[0]
                send_ref[d, 3 * QH + PER : 3 * QH + 2 * PER, :] = asks[1]
                send_ref[d, 3 * QH + 2 * PER :, :] = aux.astype(bf16)


def prepare(queries, keys, values, row, entering, lens, pick, first, shift):
    slots, kept = keys.shape[1], KVH * HD
    held = pl.BlockSpec(memory_space=pltpu.VMEM)
    small = pl.BlockSpec(memory_space=pltpu.SMEM)

    def cost(n):
        return pl.CostEstimate(flops=n, bytes_accessed=n, transcendentals=0)

    mean, fed, aux = pl.pallas_call(
        first_kernel,
        grid=(1,),
        out_shape=(
            jax.ShapeDtypeStruct((3 * QH, HD), f32),
            jax.ShapeDtypeStruct((3 * QH, HD), bf16),
            jax.ShapeDtypeStruct((2 * KVH, HD), f32),
        ),
        in_specs=[small, held, *[pl.BlockSpec((3, slots, kept), lambda i: (0, 0, 0))] * 2],
        out_specs=(held, held, held),
        scratch_shapes=[pltpu.VMEM((4 * QH, HD), f32), pltpu.VMEM((3 * QH, slots), f32)],
        cost_estimate=cost(4 << 20),
        name="first_part",
    )(lens, queries, keys, values)
    fed = shift(fed)
    late, own, tail, head, ask, aux = pl.pallas_call(
        second_kernel,
        grid=(1,),
        out_shape=(
            jax.ShapeDtypeStruct((QH, HD), f32),
            jax.ShapeDtypeStruct((2 * QH, HD), bf16),
            jax.ShapeDtypeStruct((QH, HD), bf16),
            jax.ShapeDtypeStruct((3 * QH, HD), bf16),
            jax.ShapeDtypeStruct((4 * QH, HD), bf16),
            jax.ShapeDtypeStruct((2 * KVH, HD), f32),
        ),
        in_specs=[small, small, held, *[pl.BlockSpec((1, slots, kept), lambda i: (3, 0, 0))] * 2, held, held, held],
        out_specs=(held,) * 6,
        scratch_shapes=[
            pltpu.VMEM((4 * QH, HD), f32),
            pltpu.VMEM((QH, slots), f32),
            pltpu.VMEM((2 * QH, HD), f32),
            pltpu.VMEM((6 * QH, HD), f32),
        ],
        cost_estimate=cost(16 << 20),
        name="second_part",
    )(lens, pick, queries, keys, values, row, entering, aux)
    sent = pl.pallas_call(
        third_kernel,
        out_shape=jax.ShapeDtypeStruct((16, 3 * QH + 2 * PER + 8, HD), bf16),
        in_specs=[small, held, held, held, held, held, held],
        out_specs=held,
        cost_estimate=cost(1 << 20),
        name="third_part",
    )(first, fed, head, own, tail, ask, aux)
    return sent, mean, late


def tick_kernel(tick, *refs):
    combined = tick > 0
    flags, a_ref, b_ref, ask_ref, aux_ref, turn_ref, gain_ref, here_ref, there_ref = refs[:9]
    refs = refs[9:]
    if combined:
        heard_ref, mean_ref, extra_ref = refs[:3]
        refs = refs[3:]
    if tick == 3:
        spoken, refs = refs[:3], refs[3:]
        x_ref, message_ref, scaled, both = refs
    else:
        x_ref, message_ref, scaled = refs
    half = QH * HD
    rows = x_ref.shape[0]
    first = jnp.full((rows, HD), flags[2], jnp.int32) > 0
    lane = lax.broadcasted_iota(jnp.int32, (rows, HD), 1)
    square = jnp.zeros((rows, HD), f32)
    for n in range(2 * QH):
        h = n % QH
        at = slice(h * HD, (h + 1) * HD)
        if n < QH:
            x = a_ref[:, at]
            if combined:
                if h % PER == 0:
                    g = h // PER
                    own = jnp.where(first, 0.0, heard_ref[2 * g].astype(f32))
                    new = heard_ref[2 * g + 1].astype(f32)
                mean = mean_ref[:, at].astype(f32)
                weight = own[:, h % PER : h % PER + 1]
                x = jnp.where(first, 0.0, x.astype(f32))
                x = (x + (mean + weight * (new - mean))).astype(bf16)
        else:
            x = b_ref[:, at]
            if combined:
                x = jnp.where(first, extra_ref[:, at].astype(f32), x.astype(f32)).astype(bf16)
        x_ref[:, n * HD : (n + 1) * HD] = x
        wide = x.astype(f32)
        square = square + wide * wide
        scaled[n // QH, :, at] = (wide * gain_ref[:, n * HD : (n + 1) * HD].astype(f32)).astype(bf16)
    fresh = jnp.zeros((rows, HD), f32)
    step = 2048
    for ref, part in ((here_ref, flags[0]), (there_ref, 1 - flags[0])):
        for k in range(0, half, step):
            fresh = fresh + jnp.dot(scaled[part, :, k : k + step], ref[k : k + step, :], preferred_element_type=f32)
    scale = lax.rsqrt(jnp.sum(square, axis=1, keepdims=True) / (2 * half) + 1e-05)
    fresh = fresh * scale
    key = fresh * turn_ref[0] + pltpu.roll(fresh, HD // 2, 1) * turn_ref[1]
    key = key.astype(bf16).astype(f32)
    score = jnp.zeros((rows, HD), f32)
    for i in range(PER):
        one = jnp.sum(ask_ref[:, i * HD : (i + 1) * HD].astype(f32) * key, axis=1, keepdims=True)
        score = jnp.where(lane == i, one, score)
    aux = aux_ref[:, :HD].astype(f32)
    lse = jnp.zeros((rows, HD), f32)
    for p in range(3):
        lse = lse + pltpu.roll(aux, HD - (16 + 48 * (tick // 2) + 16 * p), 1)
    own = jnp.where(lane < PER, 1.0 / (1.0 + jnp.exp(lse - score * FACTOR)), 0.0)
    is_key = jnp.full((rows, HD), flags[1], jnp.int32) > 0
    message = jnp.where(is_key, own, fresh).astype(bf16)
    if tick < 3:
        for d in range(message_ref.shape[0]):
            message_ref[d] = message
        return
    even = jnp.full((rows, HD), flags[0], jnp.int32) == 0
    both[:rows, :] = jnp.where(even, spoken[0][0].astype(f32), spoken[1][0].astype(f32))
    both[rows:, :] = jnp.where(even, spoken[2][0].astype(f32), message.astype(f32))
    for j in range(rows):
        message_ref[j] = both[pl.ds(j, 2, stride=rows), :].astype(bf16)


def do_tick(tick, flags, x, got, turn, gain, here, there, heard=None, extra=None, spoken=()):
    rows, half = got.shape[0], QH * HD
    small = pl.BlockSpec(memory_space=pltpu.SMEM)
    held = pl.BlockSpec(memory_space=pltpu.VMEM)

    def block(size, n):
        return pl.BlockSpec((rows, size), lambda i: (0, n))

    k = tick // 2
    specs = [small, block(half, 0), block(half, 1), block(PER * HD, 12 + k), block(8 * HD, 28), held, held, held, held]
    operands = [flags, x, x, got, got, turn, gain, here, there]
    if tick:
        specs += [held, block(half, 0 if tick == 3 else 2), block(half, 1)]
        operands += [heard, got, extra]
    specs += [pl.BlockSpec((1, rows, HD), lambda i: (0, 0, 0))] * len(spoken)
    operands += spoken
    return pl.pallas_call(
        functools.partial(tick_kernel, tick),
        grid=(1,),
        out_shape=(
            jax.ShapeDtypeStruct((rows, 2 * half), bf16),
            jax.ShapeDtypeStruct((rows, 2 if tick == 3 else rows, HD), bf16),
        ),
        in_specs=specs,
        out_specs=(held, held),
        scratch_shapes=[pltpu.VMEM((2, rows, half), bf16)] + [pltpu.VMEM((2 * rows, HD), f32)] * (tick == 3),
        cost_estimate=pl.CostEstimate(flops=1 << 26, bytes_accessed=6 << 20, transcendentals=0),
        compiler_params=pltpu.CompilerParams(vmem_limit_bytes=20 << 20),
    )(*operands)


def pick_kernel(flags, *refs):
    xs, (mine_ref, other_ref) = refs[:4], refs[4:]
    rows, width = xs[0].shape
    sub = lax.broadcasted_iota(jnp.int32, (8, rows), 0)
    lane = lax.broadcasted_iota(jnp.int32, (8, rows), 1)
    wanted = jnp.where(sub < 2, flags[0] * 8 + flags[3], (1 - flags[0]) * 8 + flags[3])
    selects = [jnp.where((lane == wanted) & (sub < 4) & (sub % 2 == k), 1.0, 0.0).astype(bf16) for k in range(2)]
    for r in range(2):

        @pl.when(flags[0] == r)
        def _():
            for n in range(0, width, 2048):
                at = slice(n, n + 2048)
                found = jnp.dot(selects[0], xs[r][:, at], preferred_element_type=f32)
                found = found + jnp.dot(selects[1], xs[2 + r][:, at], preferred_element_type=f32)
                mine_ref[:, at] = found[0:2].astype(bf16)
                other_ref[:, at] = found[2:4].astype(bf16)


def pick_rows(flags, *xs):
    held = pl.BlockSpec(memory_space=pltpu.VMEM)
    pair = jax.ShapeDtypeStruct((2, xs[0].shape[1]), bf16)
    return pl.pallas_call(
        pick_kernel,
        out_shape=(pair, pair),
        in_specs=[pl.BlockSpec(memory_space=pltpu.SMEM), *[held] * 4],
        out_specs=(held, held),
        cost_estimate=pl.CostEstimate(flops=1 << 20, bytes_accessed=2 << 20, transcendentals=0),
        name="pick_rows",
    )(flags, *xs)


def last_kernel(flags, mine_ref, swap_ref, told_ref, early_ref, late_ref, out_ref, tell, mean):
    mean[: 3 * QH, :] = early_ref[...]
    mean[3 * QH :, :] = late_ref[...]
    for c in range(8):
        for r in range(2):
            for k in range(2):
                t = 2 * k + r
                tell[c, t : t + 1, :] = told_ref[8 * r + c, k : k + 1, :].astype(f32)
    even = jnp.full((2, HD), flags[0], jnp.int32) == 0
    for n in range(2 * QH):
        at = slice(n * HD, (n + 1) * HD)
        mine = mine_ref[:, at].astype(f32)
        swap = swap_ref[:, at].astype(f32)
        a = jnp.where(even, mine, swap)
        b = jnp.where(even, swap, mine)
        x = jnp.concatenate([a[0:1], b[0:1], a[1:2], b[1:2]], axis=0)
        if n < QH:
            g, i = n // PER, n % PER
            cached = mean[pl.ds(n, 4, stride=QH), :]
            own = tell[2 * g][:, i : i + 1]
            x = x + (cached + own * (tell[2 * g + 1] - cached))
        out_ref[:, at] = x.astype(bf16)


def finish(flags, mine, swapped, told, early, late):
    held = pl.BlockSpec(memory_space=pltpu.VMEM)
    return pl.pallas_call(
        last_kernel,
        out_shape=jax.ShapeDtypeStruct((4, mine.shape[1]), bf16),
        in_specs=[pl.BlockSpec(memory_space=pltpu.SMEM), *[held] * 5],
        out_specs=held,
        scratch_shapes=[pltpu.VMEM((8, 4, HD), f32), pltpu.VMEM((4 * QH, HD), f32)],
        cost_estimate=pl.CostEstimate(flops=1 << 20, bytes_accessed=1 << 20, transcendentals=0),
        compiler_params=pltpu.CompilerParams(vmem_limit_bytes=8 << 20),
        name="last_part",
    )(flags, mine, swapped, told, early, late)


def inner(arriving, entering, gain, kv_weight, queries, cache_keys, cache_values, lengths):
    section_at = lax.axis_index("section")
    row_at = lax.axis_index("row")
    col_at = lax.axis_index("col")
    sections = lax.axis_size("section")
    cols = lax.axis_size("col")
    ticks = queries.shape[1]
    width = arriving.shape[2]
    half = width // 2
    last = section_at == sections - 1
    first = section_at == 0

    def at(s, r, c):
        return ((s % sections) * 2 + r) * cols + c

    def links(pairs):
        return [(at(s, r, c), at(v, w, c)) for s, r, v, w in pairs for c in range(cols)]

    def relay_group(r):
        return [
            [at(s, r, c) for c in range(cols)] + [at(s + 1, 1 - r, c) for c in range(cols)]
            for s in range(sections)
        ]

    w_here = kv_weight[0]
    w_there = lax.ppermute(w_here, "row", [(0, 1), (1, 0)])
    lens = lax.dynamic_slice_in_dim(lengths[:, 0], sections - 1 - section_at, ticks, 0)
    pick = jnp.where(first, 0, jnp.where(last, 1, 2)).astype(jnp.int32)[None]
    sent, early, late = prepare(
        queries[0, :, 0],
        cache_keys[0, :, 0],
        cache_values[0, :, 0],
        arriving[0],
        entering[:, 0],
        lens,
        pick,
        first.astype(jnp.int32)[None],
        lambda fed: lax.ppermute(fed, "section", [(s, s + 1) for s in range(sections - 1)]),
    )
    got = lax.all_to_all(sent, RC, split_axis=0, concat_axis=0, tiled=True)
    got = got.reshape(2 * cols, -1)

    aux_at = width + half + 2 * PER * HD
    turns = [jnp.stack(angles(got[:, aux_at + k].astype(f32))) for k in range(2)]
    flags = jnp.stack([row_at, 1 - col_at % 2, first.astype(jnp.int32), col_at]).astype(jnp.int32)

    rows, messages = [], []
    for tick in range(ticks):
        step = functools.partial(do_tick, tick, flags, got=got, turn=turns[tick // 2], gain=gain, here=w_here, there=w_there)
        if tick == 0:
            x, message = step(got)
        else:
            there = (tick - 1) % 2
            pairs = [(s, there, s + 1, 1 - there) for s in range(sections - 1)]
            if tick == 1:
                pairs += [(sections - 1, 1, 0, 0), (1, 1, 0, 1)]
            relayed = lax.ppermute(x, ALL, links(pairs))
            heard = lax.all_to_all(message, ALL, split_axis=0, concat_axis=0, axis_index_groups=relay_group(there), tiled=True)
            tails = relayed if tick == 1 else tails
            extra = got if tick == 1 else tails
            x, message = step(relayed, heard=heard, extra=extra, spoken=messages if tick == 3 else [])
        rows.append(x)
        messages.append(message)

    told = lax.all_to_all(messages[3], RC, split_axis=0, concat_axis=0, tiled=True)
    mine, other = pick_rows(flags, *rows)
    swapped = lax.ppermute(other, "row", [(0, 1), (1, 0)])
    out = finish(flags, mine, swapped, told, early, late)
    return out[None, :, None]


def solution(mesh):
    placed = (
        P("section", ("row", "col"), None),
        P(None, ("row", "col"), None),
        P("section", None),
        P("section", "row", "col"),
        P("section", None, ("row", "col"), None),
        P("section", None, ("row", "col"), None, None),
        P("section", None, ("row", "col"), None, None),
        P(None, ("row", "col")),
    )
    return jax.shard_map(
        inner,
        mesh=mesh,
        in_specs=placed,
        out_specs=P("section", None, ("row", "col"), None),
        check_vma=False,
    )
```

```python
import functools

import jax
import jax.numpy as jnp
import numpy as np
from jax import lax
from jax.experimental import pallas as pl
from jax.experimental.pallas import tpu as pltpu
from jax.sharding import PartitionSpec as P


QH = 64
KVH = 4
HD = 128
PER = QH // KVH
ALL = ("section", "row", "col")
RC = ("row", "col")
FACTOR = 1.0 / np.sqrt(HD)
bf16 = jnp.bfloat16
f32 = jnp.float32


def angles(positions):
    half = HD // 2
    steps_up = jnp.arange(half).astype(f32)
    inverse = jnp.exp(-jnp.log(f32(500000.0)) * steps_up / half)
    angle = positions.astype(f32)[:, None] * inverse[None, :]
    cosine = jnp.cos(angle)
    sine = jnp.sin(angle)
    return jnp.concatenate([cosine, cosine], 1), jnp.concatenate([-sine, sine], 1)


def attend(qs, k_ref, v_ref, lens, scores, ticks):
    for i, t in enumerate(ticks):
        for g in range(KVH):
            q = qs[t * QH + g * PER : t * QH + (g + 1) * PER, :].astype(bf16)
            k = k_ref[i, :, g * HD : (g + 1) * HD]
            scores[i * QH + g * PER : i * QH + (g + 1) * PER, :] = lax.dot_general(
                q, k, (((1,), (1,)), ((), ())), preferred_element_type=f32
            )
    means, lses = [], []
    lane = lax.broadcasted_iota(jnp.int32, (QH, HD), 1)
    for i, t in enumerate(ticks):
        part = scores[i * QH : (i + 1) * QH, :] * FACTOR
        part = jnp.where(lane < lens[t], part, f32(-1e30))
        top = jnp.max(part, axis=1, keepdims=True)
        weights = jnp.exp(part - top)
        total = jnp.sum(weights, axis=1, keepdims=True)
        probs = (weights / total).astype(bf16)
        lses.append(top + jnp.log(total))
        for g in range(KVH):
            v = v_ref[i, :, g * HD : (g + 1) * HD]
            means.append(jnp.dot(probs[g * PER : (g + 1) * PER], v, preferred_element_type=f32))
    return means, lses


def spread(lse, tick):
    hi = lse.astype(bf16).astype(f32)
    mid = (lse - hi).astype(bf16).astype(f32)
    low = (lse - hi) - mid
    lane = lax.broadcasted_iota(jnp.int32, (PER, HD), 1)
    row = lax.broadcasted_iota(jnp.int32, (PER, HD), 0)
    out = []
    for g in range(KVH):
        total = jnp.zeros((PER, HD), f32)
        for p, part in enumerate((hi, mid, low)):
            there = lane == row + (16 + 48 * (tick // 2) + 16 * p)
            total = total + jnp.where(there, part[g * PER : (g + 1) * PER], 0.0)
        out.append(jnp.sum(total, axis=0, keepdims=True))
    return out


def first_kernel(base, lengths, q_ref, k_ref, v_ref, mean_ref, fed_ref, aux_ref, qs, scores):
    lens = [lengths[base[0] + t] for t in range(4)]
    for h in range(QH):
        qs[pl.ds(h, 4, stride=QH), :] = q_ref[:, h * HD : (h + 1) * HD].astype(f32)
    means, lses = attend(qs, k_ref, v_ref, lens, scores, (0, 1, 2))
    for n, mean in enumerate(means):
        mean_ref[n * PER : (n + 1) * PER, :] = mean
        fed_ref[n * PER : (n + 1) * PER, :] = mean.astype(bf16)
    even, odd, late = (spread(lses[t], t) for t in (0, 1, 2))
    for g in range(KVH):
        aux_ref[g : g + 1, :] = even[g] + late[g]
        aux_ref[KVH + g : KVH + g + 1, :] = odd[g]


def second_kernel(base, lengths, pick, q_ref, k_ref, v_ref, row_ref, ent_ref, aux_in, mean_ref, own_ref, tail_ref, head_ref, ask_ref, aux_ref, qs, scores, wide, ents):
    blocks = 2 * QH
    lens = [lengths[base[0] + t] for t in range(4)]
    for h in range(QH):
        qs[pl.ds(h, 4, stride=QH), :] = q_ref[:, h * HD : (h + 1) * HD].astype(f32)
    for a in range(blocks):
        wide[a : a + 1, :] = row_ref[:, a * HD : (a + 1) * HD].astype(f32)
        ents[pl.ds(a, 3, stride=blocks), :] = ent_ref[:, a * HD : (a + 1) * HD].astype(f32)
    ask_ref[...] = qs[...].astype(bf16)
    own_ref[...] = wide[...].astype(bf16)
    chosen = pl.multiple_of(pick[0] * blocks + QH, QH)
    tail_ref[...] = ents[pl.ds(chosen, QH), :].astype(bf16)
    for t in range(3):
        head_ref[t * QH : (t + 1) * QH, :] = ents[t * blocks : t * blocks + QH, :].astype(bf16)
    means, lses = attend(qs, k_ref, v_ref, lens, scores, (3,))
    for n, mean in enumerate(means):
        mean_ref[n * PER : (n + 1) * PER, :] = mean
    late = spread(lses[0], 3)
    lane = lax.broadcasted_iota(jnp.int32, (1, HD), 1)
    for r in range(2):
        known = jnp.where(lane == 0, lens[r].astype(f32), 0.0)
        known = known + jnp.where(lane == 1, lens[2 + r].astype(f32), 0.0)
        for g in range(KVH):
            n = r * KVH + g
            row = aux_in[n : n + 1, :] + known
            aux_ref[n : n + 1, :] = row + late[g] if r else row


def third_kernel(flags, fed_ref, head_ref, own_ref, tail_ref, ask_ref, aux_ref, send_ref):
    first = jnp.full((3 * QH, HD), flags[0], jnp.int32) > 0
    fed = jnp.where(first, head_ref[...].astype(f32), fed_ref[...].astype(f32)).astype(bf16)
    own = own_ref[...]
    tail = tail_ref[...]
    pad = jnp.zeros((8, HD), f32)
    sub = lax.broadcasted_iota(jnp.int32, (8, HD), 0)
    for g in range(KVH):
        for r in range(2):
            aux = jnp.where(sub == 0, jnp.broadcast_to(aux_ref[r * KVH + g : r * KVH + g + 1, :], (8, HD)), pad)
            asks = [ask_ref[t * QH + g * PER : t * QH + (g + 1) * PER, :] for t in (r, 2 + r)]
            for c in (2 * g, 2 * g + 1):
                d = 8 * r + c
                if r == 0:
                    send_ref[d, : 2 * QH, :] = own
                    send_ref[d, 2 * QH : 3 * QH, :] = fed[QH : 2 * QH]
                else:
                    send_ref[d, :QH, :] = fed[2 * QH :]
                    send_ref[d, QH : 2 * QH, :] = tail
                    send_ref[d, 2 * QH : 3 * QH, :] = fed[:QH]
                send_ref[d, 3 * QH : 3 * QH + PER, :] = asks[0]
                send_ref[d, 3 * QH + PER : 3 * QH + 2 * PER, :] = asks[1]
                send_ref[d, 3 * QH + 2 * PER :, :] = aux.astype(bf16)


def prepare(queries, keys, values, row, entering, base, lengths, pick, first, shift):
    slots, kept = keys.shape[1], KVH * HD
    held = pl.BlockSpec(memory_space=pltpu.VMEM)
    small = pl.BlockSpec(memory_space=pltpu.SMEM)

    def cost(n):
        return pl.CostEstimate(flops=n, bytes_accessed=n, transcendentals=0)

    mean, fed, aux = pl.pallas_call(
        first_kernel,
        grid=(1,),
        out_shape=(
            jax.ShapeDtypeStruct((3 * QH, HD), f32),
            jax.ShapeDtypeStruct((3 * QH, HD), bf16),
            jax.ShapeDtypeStruct((2 * KVH, HD), f32),
        ),
        in_specs=[small, small, held, *[pl.BlockSpec((3, slots, kept), lambda i: (0, 0, 0))] * 2],
        out_specs=(held, held, held),
        scratch_shapes=[pltpu.VMEM((4 * QH, HD), f32), pltpu.VMEM((3 * QH, slots), f32)],
        cost_estimate=cost(4 << 20),
        name="first_part",
    )(base, lengths, queries, keys, values)
    fed = shift(fed)
    late, own, tail, head, ask, aux = pl.pallas_call(
        second_kernel,
        grid=(1,),
        out_shape=(
            jax.ShapeDtypeStruct((QH, HD), f32),
            jax.ShapeDtypeStruct((2 * QH, HD), bf16),
            jax.ShapeDtypeStruct((QH, HD), bf16),
            jax.ShapeDtypeStruct((3 * QH, HD), bf16),
            jax.ShapeDtypeStruct((4 * QH, HD), bf16),
            jax.ShapeDtypeStruct((2 * KVH, HD), f32),
        ),
        in_specs=[small, small, small, held, *[pl.BlockSpec((1, slots, kept), lambda i: (3, 0, 0))] * 2, held, held, held],
        out_specs=(held,) * 6,
        scratch_shapes=[
            pltpu.VMEM((4 * QH, HD), f32),
            pltpu.VMEM((QH, slots), f32),
            pltpu.VMEM((2 * QH, HD), f32),
            pltpu.VMEM((6 * QH, HD), f32),
        ],
        cost_estimate=cost(16 << 20),
        name="second_part",
    )(base, lengths, pick, queries, keys, values, row, entering, aux)
    sent = pl.pallas_call(
        third_kernel,
        out_shape=jax.ShapeDtypeStruct((16, 3 * QH + 2 * PER + 8, HD), bf16),
        in_specs=[small, held, held, held, held, held, held],
        out_specs=held,
        cost_estimate=cost(1 << 20),
        name="third_part",
    )(first, fed, head, own, tail, ask, aux)
    return sent, mean, late


def tick_kernel(tick, *refs):
    combined = tick > 0
    flags, a_ref, b_ref, ask_ref, aux_ref, turn_ref, gain_ref, here_ref, there_ref = refs[:9]
    refs = refs[9:]
    if combined:
        heard_ref, mean_ref, extra_ref = refs[:3]
        refs = refs[3:]
    if tick == 3:
        spoken, refs = refs[:3], refs[3:]
        x_ref, message_ref, scaled, held_there, arrived, both = refs
    else:
        x_ref, message_ref, scaled, held_there, arrived = refs
    bring = pltpu.make_async_copy(there_ref, held_there, arrived)
    bring.start()
    half = QH * HD
    rows = x_ref.shape[0]
    first = jnp.full((rows, HD), flags[2], jnp.int32) > 0
    lane = lax.broadcasted_iota(jnp.int32, (rows, HD), 1)
    square = jnp.zeros((rows, HD), f32)
    for n in range(2 * QH):
        h = n % QH
        at = slice(h * HD, (h + 1) * HD)
        if n < QH:
            x = a_ref[:, at]
            if combined:
                if h % PER == 0:
                    g = h // PER
                    own = jnp.where(first, 0.0, heard_ref[2 * g].astype(f32))
                    new = heard_ref[2 * g + 1].astype(f32)
                mean = mean_ref[:, at].astype(f32)
                weight = own[:, h % PER : h % PER + 1]
                x = jnp.where(first, 0.0, x.astype(f32))
                x = (x + (mean + weight * (new - mean))).astype(bf16)
        else:
            x = b_ref[:, at]
            if combined:
                x = jnp.where(first, extra_ref[:, at].astype(f32), x.astype(f32)).astype(bf16)
        x_ref[:, n * HD : (n + 1) * HD] = x
        wide = x.astype(f32)
        square = square + wide * wide
        scaled[n // QH, :, at] = (wide * gain_ref[:, n * HD : (n + 1) * HD].astype(f32)).astype(bf16)
    fresh = jnp.zeros((rows, HD), f32)
    step = 2048
    for ref, part in ((here_ref, flags[0]), (held_there, 1 - flags[0])):
        if ref is held_there:
            bring.wait()
        for k in range(0, half, step):
            fresh = fresh + jnp.dot(scaled[part, :, k : k + step], ref[k : k + step, :], preferred_element_type=f32)
    scale = lax.rsqrt(jnp.sum(square, axis=1, keepdims=True) / (2 * half) + 1e-05)
    fresh = fresh * scale
    k = tick // 2
    key = fresh * turn_ref[2 * k] + pltpu.roll(fresh, HD // 2, 1) * turn_ref[2 * k + 1]
    key = key.astype(bf16).astype(f32)
    score = jnp.zeros((rows, HD), f32)
    for i in range(PER):
        one = jnp.sum(ask_ref[:, i * HD : (i + 1) * HD].astype(f32) * key, axis=1, keepdims=True)
        score = jnp.where(lane == i, one, score)
    aux = aux_ref[:, :HD].astype(f32)
    lse = jnp.zeros((rows, HD), f32)
    for p in range(3):
        lse = lse + pltpu.roll(aux, HD - (16 + 48 * (tick // 2) + 16 * p), 1)
    own = jnp.where(lane < PER, 1.0 / (1.0 + jnp.exp(lse - score * FACTOR)), 0.0)
    is_key = jnp.full((rows, HD), flags[1], jnp.int32) > 0
    message = jnp.where(is_key, own, fresh).astype(bf16)
    if tick < 3:
        for d in range(message_ref.shape[0]):
            message_ref[d] = message
        return
    even = jnp.full((rows, HD), flags[0], jnp.int32) == 0
    both[:rows, :] = jnp.where(even, spoken[0][0].astype(f32), spoken[1][0].astype(f32))
    both[rows:, :] = jnp.where(even, spoken[2][0].astype(f32), message.astype(f32))
    for j in range(rows):
        message_ref[j] = both[pl.ds(j, 2, stride=rows), :].astype(bf16)


def do_tick(tick, flags, x, got, turn, gain, here, there, heard=None, extra=None, spoken=()):
    rows, half = got.shape[0], QH * HD
    small = pl.BlockSpec(memory_space=pltpu.SMEM)
    held = pl.BlockSpec(memory_space=pltpu.VMEM)

    def block(size, n):
        return pl.BlockSpec((rows, size), lambda i: (0, n))

    k = tick // 2
    specs = [small, block(half, 0), block(half, 1), block(PER * HD, 12 + k), block(8 * HD, 28), held, held, held, pl.BlockSpec(memory_space=pl.ANY)]
    operands = [flags, x, x, got, got, turn, gain, here, there]
    if tick:
        specs += [held, block(half, 0 if tick == 3 else 2), block(half, 1)]
        operands += [heard, got, extra]
    specs += [pl.BlockSpec((1, rows, HD), lambda i: (0, 0, 0))] * len(spoken)
    operands += spoken
    return pl.pallas_call(
        functools.partial(tick_kernel, tick),
        grid=(1,),
        out_shape=(
            jax.ShapeDtypeStruct((rows, 2 * half), bf16),
            jax.ShapeDtypeStruct((rows, 2 if tick == 3 else rows, HD), bf16),
        ),
        in_specs=specs,
        out_specs=(held, held),
        scratch_shapes=[
            pltpu.VMEM((2, rows, half), bf16),
            pltpu.VMEM(there.shape, bf16),
            pltpu.SemaphoreType.DMA,
            *[pltpu.VMEM((2 * rows, HD), f32)] * (tick == 3),
        ],
        cost_estimate=pl.CostEstimate(flops=1 << 26, bytes_accessed=6 << 20, transcendentals=0),
        compiler_params=pltpu.CompilerParams(vmem_limit_bytes=20 << 20),
    )(*operands)


def pick_kernel(flags, *refs):
    xs, (mine_ref, other_ref) = refs[:4], refs[4:]
    rows, width = xs[0].shape
    sub = lax.broadcasted_iota(jnp.int32, (8, rows), 0)
    lane = lax.broadcasted_iota(jnp.int32, (8, rows), 1)
    wanted = jnp.where(sub < 2, flags[0] * 8 + flags[3], (1 - flags[0]) * 8 + flags[3])
    selects = [jnp.where((lane == wanted) & (sub < 4) & (sub % 2 == k), 1.0, 0.0).astype(bf16) for k in range(2)]
    for r in range(2):

        @pl.when(flags[0] == r)
        def _():
            for n in range(0, width, 2048):
                at = slice(n, n + 2048)
                found = jnp.dot(selects[0], xs[r][:, at], preferred_element_type=f32)
                found = found + jnp.dot(selects[1], xs[2 + r][:, at], preferred_element_type=f32)
                mine_ref[:, at] = found[0:2].astype(bf16)
                other_ref[:, at] = found[2:4].astype(bf16)


def pick_rows(flags, *xs):
    held = pl.BlockSpec(memory_space=pltpu.VMEM)
    pair = jax.ShapeDtypeStruct((2, xs[0].shape[1]), bf16)
    return pl.pallas_call(
        pick_kernel,
        out_shape=(pair, pair),
        in_specs=[pl.BlockSpec(memory_space=pltpu.SMEM), *[held] * 4],
        out_specs=(held, held),
        cost_estimate=pl.CostEstimate(flops=1 << 20, bytes_accessed=2 << 20, transcendentals=0),
        name="pick_rows",
    )(flags, *xs)


def last_kernel(flags, mine_ref, swap_ref, told_ref, early_ref, late_ref, out_ref, tell, mean):
    mean[: 3 * QH, :] = early_ref[...]
    mean[3 * QH :, :] = late_ref[...]
    for c in range(8):
        for r in range(2):
            for k in range(2):
                t = 2 * k + r
                tell[c, t : t + 1, :] = told_ref[8 * r + c, k : k + 1, :].astype(f32)
    even = jnp.full((2, HD), flags[0], jnp.int32) == 0
    for n in range(2 * QH):
        at = slice(n * HD, (n + 1) * HD)
        mine = mine_ref[:, at].astype(f32)
        swap = swap_ref[:, at].astype(f32)
        a = jnp.where(even, mine, swap)
        b = jnp.where(even, swap, mine)
        x = jnp.concatenate([a[0:1], b[0:1], a[1:2], b[1:2]], axis=0)
        if n < QH:
            g, i = n // PER, n % PER
            cached = mean[pl.ds(n, 4, stride=QH), :]
            own = tell[2 * g][:, i : i + 1]
            x = x + (cached + own * (tell[2 * g + 1] - cached))
        out_ref[:, at] = x.astype(bf16)


def finish(flags, mine, swapped, told, early, late):
    held = pl.BlockSpec(memory_space=pltpu.VMEM)
    return pl.pallas_call(
        last_kernel,
        out_shape=jax.ShapeDtypeStruct((4, mine.shape[1]), bf16),
        in_specs=[pl.BlockSpec(memory_space=pltpu.SMEM), *[held] * 5],
        out_specs=held,
        scratch_shapes=[pltpu.VMEM((8, 4, HD), f32), pltpu.VMEM((4 * QH, HD), f32)],
        cost_estimate=pl.CostEstimate(flops=1 << 20, bytes_accessed=1 << 20, transcendentals=0),
        compiler_params=pltpu.CompilerParams(vmem_limit_bytes=8 << 20),
        name="last_part",
    )(flags, mine, swapped, told, early, late)


def inner(arriving, entering, gain, kv_weight, queries, cache_keys, cache_values, lengths):
    section_at = lax.axis_index("section")
    row_at = lax.axis_index("row")
    col_at = lax.axis_index("col")
    sections = lax.axis_size("section")
    cols = lax.axis_size("col")
    ticks = queries.shape[1]
    width = arriving.shape[2]
    half = width // 2
    last = section_at == sections - 1
    first = section_at == 0

    def at(s, r, c):
        return ((s % sections) * 2 + r) * cols + c

    def links(pairs):
        return [(at(s, r, c), at(v, w, c)) for s, r, v, w in pairs for c in range(cols)]

    def relay_group(r):
        return [
            [at(s, r, c) for c in range(cols)] + [at(s + 1, 1 - r, c) for c in range(cols)]
            for s in range(sections)
        ]

    w_here = kv_weight[0]
    w_there = lax.ppermute(w_here, "row", [(0, 1), (1, 0)])
    pick = jnp.where(first, 0, jnp.where(last, 1, 2)).astype(jnp.int32)[None]
    sent, early, late = prepare(
        queries[0, :, 0],
        cache_keys[0, :, 0],
        cache_values[0, :, 0],
        arriving[0],
        entering[:, 0],
        (sections - 1 - section_at).astype(jnp.int32)[None],
        lengths[:, 0],
        pick,
        first.astype(jnp.int32)[None],
        lambda fed: lax.ppermute(fed, "section", [(s, s + 1) for s in range(sections - 1)]),
    )
    got = lax.all_to_all(sent, RC, split_axis=0, concat_axis=0, tiled=True)
    got = got.reshape(2 * cols, -1)

    aux_at = width + half + 2 * PER * HD
    turns = jnp.stack([t for k in range(2) for t in angles(got[:, aux_at + k].astype(f32))])
    flags = jnp.stack([row_at, 1 - col_at % 2, first.astype(jnp.int32), col_at]).astype(jnp.int32)

    rows, messages = [], []
    for tick in range(ticks):
        step = functools.partial(do_tick, tick, flags, got=got, turn=turns, gain=gain, here=w_here, there=w_there)
        if tick == 0:
            x, message = step(got)
        else:
            there = (tick - 1) % 2
            pairs = [(s, there, s + 1, 1 - there) for s in range(sections - 1)]
            relayed = lax.ppermute(x, ALL, links(pairs))
            heard = lax.all_to_all(message, ALL, split_axis=0, concat_axis=0, axis_index_groups=relay_group(there), tiled=True)
            if tick == 1:
                tails = lax.ppermute(x, ALL, links([(sections - 1, 1, 0, 0), (1, 1, 0, 1)]))
            extra = got if tick == 1 else tails
            x, message = step(relayed, heard=heard, extra=extra, spoken=messages if tick == 3 else [])
        rows.append(x)
        messages.append(message)

    told = lax.all_to_all(messages[3], RC, split_axis=0, concat_axis=0, tiled=True)
    mine, other = pick_rows(flags, *rows)
    swapped = lax.ppermute(other, "row", [(0, 1), (1, 0)])
    out = finish(flags, mine, swapped, told, early, late)
    return out[None, :, None]


def solution(mesh):
    placed = (
        P("section", ("row", "col"), None),
        P(None, ("row", "col"), None),
        P("section", None),
        P("section", "row", "col"),
        P("section", None, ("row", "col"), None),
        P("section", None, ("row", "col"), None, None),
        P("section", None, ("row", "col"), None, None),
        P(None, ("row", "col")),
    )
    return jax.shard_map(
        inner,
        mesh=mesh,
        in_specs=placed,
        out_specs=P("section", None, ("row", "col"), None),
        check_vma=False,
    )
```

```python
import functools

import jax
import jax.numpy as jnp
import numpy as np
from jax import lax
from jax.experimental import pallas as pl
from jax.experimental.pallas import tpu as pltpu
from jax.sharding import PartitionSpec as P


QH = 64
KVH = 4
HD = 128
PER = QH // KVH
ALL = ("section", "row", "col")
RC = ("row", "col")
FACTOR = 1.0 / np.sqrt(HD)
bf16 = jnp.bfloat16
f32 = jnp.float32


def angles(positions):
    half = HD // 2
    steps_up = jnp.arange(half).astype(f32)
    inverse = jnp.exp(-jnp.log(f32(500000.0)) * steps_up / half)
    angle = positions.astype(f32)[:, None] * inverse[None, :]
    cosine = jnp.cos(angle)
    sine = jnp.sin(angle)
    return jnp.concatenate([cosine, cosine], 1), jnp.concatenate([-sine, sine], 1)


def attend(qs, k_ref, v_ref, lens, scores, ticks):
    for i, t in enumerate(ticks):
        for g in range(KVH):
            q = qs[t * QH + g * PER : t * QH + (g + 1) * PER, :].astype(bf16)
            k = k_ref[i, :, g * HD : (g + 1) * HD]
            scores[i * QH + g * PER : i * QH + (g + 1) * PER, :] = lax.dot_general(
                q, k, (((1,), (1,)), ((), ())), preferred_element_type=f32
            )
    means, lses = [], []
    lane = lax.broadcasted_iota(jnp.int32, (QH, HD), 1)
    for i, t in enumerate(ticks):
        part = scores[i * QH : (i + 1) * QH, :] * FACTOR
        part = jnp.where(lane < lens[t], part, f32(-1e30))
        top = jnp.max(part, axis=1, keepdims=True)
        weights = jnp.exp(part - top)
        total = jnp.sum(weights, axis=1, keepdims=True)
        probs = (weights / total).astype(bf16)
        lses.append(top + jnp.log(total))
        for g in range(KVH):
            v = v_ref[i, :, g * HD : (g + 1) * HD]
            means.append(jnp.dot(probs[g * PER : (g + 1) * PER], v, preferred_element_type=f32))
    return means, lses


def spread(lse, tick):
    hi = lse.astype(bf16).astype(f32)
    mid = (lse - hi).astype(bf16).astype(f32)
    low = (lse - hi) - mid
    lane = lax.broadcasted_iota(jnp.int32, (PER, HD), 1)
    row = lax.broadcasted_iota(jnp.int32, (PER, HD), 0)
    out = []
    for g in range(KVH):
        total = jnp.zeros((PER, HD), f32)
        for p, part in enumerate((hi, mid, low)):
            there = lane == row + (16 + 48 * (tick // 2) + 16 * p)
            total = total + jnp.where(there, part[g * PER : (g + 1) * PER], 0.0)
        out.append(jnp.sum(total, axis=0, keepdims=True))
    return out


def first_kernel(base, lengths, q_ref, k_ref, v_ref, mean_ref, fed_ref, aux_ref, qs, scores):
    lens = [lengths[base[0] + t] for t in range(4)]
    for h in range(QH):
        qs[pl.ds(h, 4, stride=QH), :] = q_ref[:, h * HD : (h + 1) * HD].astype(f32)
    means, lses = attend(qs, k_ref, v_ref, lens, scores, (0, 1, 2))
    for n, mean in enumerate(means):
        mean_ref[n * PER : (n + 1) * PER, :] = mean
        fed_ref[n * PER : (n + 1) * PER, :] = mean.astype(bf16)
    even, odd, late = (spread(lses[t], t) for t in (0, 1, 2))
    for g in range(KVH):
        aux_ref[g : g + 1, :] = even[g] + late[g]
        aux_ref[KVH + g : KVH + g + 1, :] = odd[g]


def second_kernel(base, lengths, pick, q_ref, k_ref, v_ref, row_ref, ent_ref, aux_in, mean_ref, own_ref, tail_ref, head_ref, ask_ref, aux_ref, qs, scores, wide, ents):
    blocks = 2 * QH
    lens = [lengths[base[0] + t] for t in range(4)]
    for h in range(QH):
        qs[pl.ds(h, 4, stride=QH), :] = q_ref[:, h * HD : (h + 1) * HD].astype(f32)
    for a in range(blocks):
        wide[a : a + 1, :] = row_ref[:, a * HD : (a + 1) * HD].astype(f32)
        ents[pl.ds(a, 3, stride=blocks), :] = ent_ref[:, a * HD : (a + 1) * HD].astype(f32)
    ask_ref[...] = qs[...].astype(bf16)
    own_ref[...] = wide[...].astype(bf16)
    chosen = pl.multiple_of(pick[0] * blocks + QH, QH)
    tail_ref[...] = ents[pl.ds(chosen, QH), :].astype(bf16)
    for t in range(3):
        head_ref[t * QH : (t + 1) * QH, :] = ents[t * blocks : t * blocks + QH, :].astype(bf16)
    means, lses = attend(qs, k_ref, v_ref, lens, scores, (3,))
    for n, mean in enumerate(means):
        mean_ref[n * PER : (n + 1) * PER, :] = mean
    late = spread(lses[0], 3)
    lane = lax.broadcasted_iota(jnp.int32, (1, HD), 1)
    for r in range(2):
        known = jnp.where(lane == 0, lens[r].astype(f32), 0.0)
        known = known + jnp.where(lane == 1, lens[2 + r].astype(f32), 0.0)
        for g in range(KVH):
            n = r * KVH + g
            row = aux_in[n : n + 1, :] + known
            aux_ref[n : n + 1, :] = row + late[g] if r else row


def third_kernel(flags, fed_ref, head_ref, own_ref, tail_ref, ask_ref, aux_ref, send_ref):
    first = jnp.full((3 * QH, HD), flags[0], jnp.int32) > 0
    fed = jnp.where(first, head_ref[...].astype(f32), fed_ref[...].astype(f32)).astype(bf16)
    own = own_ref[...]
    tail = tail_ref[...]
    pad = jnp.zeros((8, HD), f32)
    sub = lax.broadcasted_iota(jnp.int32, (8, HD), 0)
    for g in range(KVH):
        for r in range(2):
            aux = jnp.where(sub == 0, jnp.broadcast_to(aux_ref[r * KVH + g : r * KVH + g + 1, :], (8, HD)), pad)
            asks = [ask_ref[t * QH + g * PER : t * QH + (g + 1) * PER, :] for t in (r, 2 + r)]
            for c in (2 * g, 2 * g + 1):
                d = 8 * r + c
                if r == 0:
                    send_ref[d, : 2 * QH, :] = own
                    send_ref[d, 2 * QH : 3 * QH, :] = fed[QH : 2 * QH]
                else:
                    send_ref[d, :QH, :] = fed[2 * QH :]
                    send_ref[d, QH : 2 * QH, :] = tail
                    send_ref[d, 2 * QH : 3 * QH, :] = fed[:QH]
                send_ref[d, 3 * QH : 3 * QH + PER, :] = asks[0]
                send_ref[d, 3 * QH + PER : 3 * QH + 2 * PER, :] = asks[1]
                send_ref[d, 3 * QH + 2 * PER :, :] = aux.astype(bf16)


def prepare(queries, keys, values, row, entering, base, lengths, pick, first, shift):
    slots, kept = keys.shape[1], KVH * HD
    held = pl.BlockSpec(memory_space=pltpu.VMEM)
    small = pl.BlockSpec(memory_space=pltpu.SMEM)

    def cost(n):
        return pl.CostEstimate(flops=n, bytes_accessed=n, transcendentals=0)

    mean, fed, aux = pl.pallas_call(
        first_kernel,
        grid=(1,),
        out_shape=(
            jax.ShapeDtypeStruct((3 * QH, HD), f32),
            jax.ShapeDtypeStruct((3 * QH, HD), bf16),
            jax.ShapeDtypeStruct((2 * KVH, HD), f32),
        ),
        in_specs=[small, small, held, *[pl.BlockSpec((3, slots, kept), lambda i: (0, 0, 0))] * 2],
        out_specs=(held, held, held),
        scratch_shapes=[pltpu.VMEM((4 * QH, HD), f32), pltpu.VMEM((3 * QH, slots), f32)],
        cost_estimate=cost(4 << 20),
        name="first_part",
    )(base, lengths, queries, keys, values)
    fed = shift(fed)
    late, own, tail, head, ask, aux = pl.pallas_call(
        second_kernel,
        grid=(1,),
        out_shape=(
            jax.ShapeDtypeStruct((QH, HD), f32),
            jax.ShapeDtypeStruct((2 * QH, HD), bf16),
            jax.ShapeDtypeStruct((QH, HD), bf16),
            jax.ShapeDtypeStruct((3 * QH, HD), bf16),
            jax.ShapeDtypeStruct((4 * QH, HD), bf16),
            jax.ShapeDtypeStruct((2 * KVH, HD), f32),
        ),
        in_specs=[small, small, small, held, *[pl.BlockSpec((1, slots, kept), lambda i: (3, 0, 0))] * 2, held, held, held],
        out_specs=(held,) * 6,
        scratch_shapes=[
            pltpu.VMEM((4 * QH, HD), f32),
            pltpu.VMEM((QH, slots), f32),
            pltpu.VMEM((2 * QH, HD), f32),
            pltpu.VMEM((6 * QH, HD), f32),
        ],
        cost_estimate=cost(16 << 20),
        name="second_part",
    )(base, lengths, pick, queries, keys, values, row, entering, aux)
    sent = pl.pallas_call(
        third_kernel,
        out_shape=jax.ShapeDtypeStruct((16, 3 * QH + 2 * PER + 8, HD), bf16),
        in_specs=[small, held, held, held, held, held, held],
        out_specs=held,
        cost_estimate=cost(1 << 20),
        name="third_part",
    )(first, fed, head, own, tail, ask, aux)
    return sent, mean, late


def tick_kernel(tick, *refs):
    combined = tick > 0
    flags, a_ref, b_ref, ask_ref, aux_ref, turn_ref, gain_ref, here_ref, there_ref = refs[:9]
    refs = refs[9:]
    if combined:
        heard_ref, mean_ref, extra_ref = refs[:3]
        refs = refs[3:]
    if tick == 3:
        spoken, found, refs = refs[:3], refs[3:6], refs[6:]
        x_ref, message_ref, pick_ref, scaled, exact, both = refs
    else:
        x_ref, message_ref, pick_ref, scaled, exact = refs
    half = QH * HD
    rows = x_ref.shape[0]
    first = jnp.full((rows, HD), flags[2], jnp.int32) > 0
    lane = lax.broadcasted_iota(jnp.int32, (rows, HD), 1)
    square = jnp.zeros((rows, HD), f32)
    for n in range(2 * QH):
        h = n % QH
        at = slice(h * HD, (h + 1) * HD)
        if n < QH:
            x = a_ref[:, at]
            if combined:
                if h % PER == 0:
                    g = h // PER
                    own = jnp.where(first, 0.0, heard_ref[2 * g].astype(f32))
                    new = heard_ref[2 * g + 1].astype(f32)
                mean = mean_ref[:, at].astype(f32)
                weight = own[:, h % PER : h % PER + 1]
                x = jnp.where(first, 0.0, x.astype(f32))
                x = (x + (mean + weight * (new - mean))).astype(bf16)
        else:
            x = b_ref[:, at]
            if combined:
                x = jnp.where(first, extra_ref[:, at].astype(f32), x.astype(f32)).astype(bf16)
        x_ref[:, n * HD : (n + 1) * HD] = x
        wide = x.astype(f32)
        exact[n * rows : (n + 1) * rows, :] = wide
        square = square + wide * wide
        scaled[n // QH, :, at] = (wide * gain_ref[:, n * HD : (n + 1) * HD].astype(f32)).astype(bf16)
    fresh = jnp.zeros((rows, HD), f32)
    step = 2048
    for ref, part in ((here_ref, flags[0]), (there_ref, 1 - flags[0])):
        for k in range(0, half, step):
            fresh = fresh + jnp.dot(scaled[part, :, k : k + step], ref[k : k + step, :], preferred_element_type=f32)
    scale = lax.rsqrt(jnp.sum(square, axis=1, keepdims=True) / (2 * half) + 1e-05)
    fresh = fresh * scale
    k = tick // 2
    key = fresh * turn_ref[2 * k] + pltpu.roll(fresh, HD // 2, 1) * turn_ref[2 * k + 1]
    key = key.astype(bf16).astype(f32)
    score = jnp.zeros((rows, HD), f32)
    for i in range(PER):
        one = jnp.sum(ask_ref[:, i * HD : (i + 1) * HD].astype(f32) * key, axis=1, keepdims=True)
        score = jnp.where(lane == i, one, score)
    aux = aux_ref[:, :HD].astype(f32)
    lse = jnp.zeros((rows, HD), f32)
    for p in range(3):
        lse = lse + pltpu.roll(aux, HD - (16 + 48 * (tick // 2) + 16 * p), 1)
    own = jnp.where(lane < PER, 1.0 / (1.0 + jnp.exp(lse - score * FACTOR)), 0.0)
    is_key = jnp.full((rows, HD), flags[1], jnp.int32) > 0
    message = jnp.where(is_key, own, fresh).astype(bf16)
    even = jnp.full((2, HD), flags[0], jnp.int32) == 0
    for n in range(2 * QH):
        at = slice(n * HD, (n + 1) * HD)
        pair = exact[pl.ds(n * rows + flags[3], 2, stride=rows // 2), :]
        if tick == 3:
            early = jnp.where(even, found[0][:, at].astype(f32), found[1][:, at].astype(f32))
            late = jnp.where(even, found[2][:, at].astype(f32), pair)
            pair = jnp.concatenate([early, late], axis=0)
        pick_ref[:, at] = pair.astype(bf16)
    if tick < 3:
        for d in range(message_ref.shape[0]):
            message_ref[d] = message
        return
    even = jnp.full((rows, HD), flags[0], jnp.int32) == 0
    both[:rows, :] = jnp.where(even, spoken[0][0].astype(f32), spoken[1][0].astype(f32))
    both[rows:, :] = jnp.where(even, spoken[2][0].astype(f32), message.astype(f32))
    for j in range(rows):
        message_ref[j] = both[pl.ds(j, 2, stride=rows), :].astype(bf16)


def do_tick(tick, flags, x, got, turn, gain, here, there, heard=None, extra=None, spoken=(), found=()):
    rows, half = got.shape[0], QH * HD
    small = pl.BlockSpec(memory_space=pltpu.SMEM)
    held = pl.BlockSpec(memory_space=pltpu.VMEM)

    def block(size, n):
        return pl.BlockSpec((rows, size), lambda i: (0, n))

    k = tick // 2
    specs = [small, block(half, 0), block(half, 1), block(PER * HD, 12 + k), block(8 * HD, 28), held, held, held, held]
    operands = [flags, x, x, got, got, turn, gain, here, there]
    if tick:
        specs += [held, block(half, 0 if tick == 3 else 2), block(half, 1)]
        operands += [heard, got, extra]
    specs += [pl.BlockSpec((1, rows, HD), lambda i: (0, 0, 0))] * len(spoken)
    operands += spoken
    specs += [held] * len(found)
    operands += found
    return pl.pallas_call(
        functools.partial(tick_kernel, tick),
        grid=(1,),
        out_shape=(
            jax.ShapeDtypeStruct((rows, 2 * half), bf16),
            jax.ShapeDtypeStruct((rows, 2 if tick == 3 else rows, HD), bf16),
            jax.ShapeDtypeStruct((4 if tick == 3 else 2, 2 * half), bf16),
        ),
        in_specs=specs,
        out_specs=(held, held, held),
        scratch_shapes=[
            pltpu.VMEM((2, rows, half), bf16),
            pltpu.VMEM((2 * QH * rows, HD), f32),
            *[pltpu.VMEM((2 * rows, HD), f32)] * (tick == 3),
        ],
        cost_estimate=pl.CostEstimate(flops=1 << 26, bytes_accessed=6 << 20, transcendentals=0),
        compiler_params=pltpu.CompilerParams(vmem_limit_bytes=20 << 20),
    )(*operands)


def last_kernel(flags, mine_ref, swap_ref, told_ref, early_ref, late_ref, out_ref, tell, mean):
    mean[: 3 * QH, :] = early_ref[...]
    mean[3 * QH :, :] = late_ref[...]
    for c in range(8):
        for r in range(2):
            for k in range(2):
                t = 2 * k + r
                tell[c, t : t + 1, :] = told_ref[8 * r + c, k : k + 1, :].astype(f32)
    even = jnp.full((4, HD), flags[0], jnp.int32) == 0
    for n in range(2 * QH):
        at = slice(n * HD, (n + 1) * HD)
        e = mine_ref[:, at].astype(f32)
        f = swap_ref[:, at].astype(f32)
        a = jnp.concatenate([e[0:1], f[0:1], e[2:3], f[2:3]], axis=0)
        b = jnp.concatenate([f[1:2], e[1:2], f[3:4], e[3:4]], axis=0)
        x = jnp.where(even, a, b)
        if n < QH:
            g, i = n // PER, n % PER
            cached = mean[pl.ds(n, 4, stride=QH), :]
            own = tell[2 * g][:, i : i + 1]
            x = x + (cached + own * (tell[2 * g + 1] - cached))
        out_ref[:, at] = x.astype(bf16)


def finish(flags, mine, swapped, told, early, late):
    held = pl.BlockSpec(memory_space=pltpu.VMEM)
    return pl.pallas_call(
        last_kernel,
        out_shape=jax.ShapeDtypeStruct((4, mine.shape[1]), bf16),
        in_specs=[pl.BlockSpec(memory_space=pltpu.SMEM), *[held] * 5],
        out_specs=held,
        scratch_shapes=[pltpu.VMEM((8, 4, HD), f32), pltpu.VMEM((4 * QH, HD), f32)],
        cost_estimate=pl.CostEstimate(flops=1 << 20, bytes_accessed=1 << 20, transcendentals=0),
        compiler_params=pltpu.CompilerParams(vmem_limit_bytes=8 << 20),
        name="last_part",
    )(flags, mine, swapped, told, early, late)


def inner(arriving, entering, gain, kv_weight, queries, cache_keys, cache_values, lengths):
    section_at = lax.axis_index("section")
    row_at = lax.axis_index("row")
    col_at = lax.axis_index("col")
    sections = lax.axis_size("section")
    cols = lax.axis_size("col")
    ticks = queries.shape[1]
    width = arriving.shape[2]
    half = width // 2
    last = section_at == sections - 1
    first = section_at == 0

    def at(s, r, c):
        return ((s % sections) * 2 + r) * cols + c

    def links(pairs):
        return [(at(s, r, c), at(v, w, c)) for s, r, v, w in pairs for c in range(cols)]

    def relay_group(r):
        return [
            [at(s, r, c) for c in range(cols)] + [at(s + 1, 1 - r, c) for c in range(cols)]
            for s in range(sections)
        ]

    w_here = kv_weight[0]
    w_there = lax.ppermute(w_here, "row", [(0, 1), (1, 0)])
    pick = jnp.where(first, 0, jnp.where(last, 1, 2)).astype(jnp.int32)[None]
    sent, early, late = prepare(
        queries[0, :, 0],
        cache_keys[0, :, 0],
        cache_values[0, :, 0],
        arriving[0],
        entering[:, 0],
        (sections - 1 - section_at).astype(jnp.int32)[None],
        lengths[:, 0],
        pick,
        first.astype(jnp.int32)[None],
        lambda fed: lax.ppermute(fed, "section", [(s, s + 1) for s in range(sections - 1)]),
    )
    got = lax.all_to_all(sent, RC, split_axis=0, concat_axis=0, tiled=True)
    got = got.reshape(2 * cols, -1)

    aux_at = width + half + 2 * PER * HD
    turns = jnp.stack([t for k in range(2) for t in angles(got[:, aux_at + k].astype(f32))])
    flags = jnp.stack([row_at, 1 - col_at % 2, first.astype(jnp.int32), col_at]).astype(jnp.int32)

    found, messages = [], []
    for tick in range(ticks):
        step = functools.partial(do_tick, tick, flags, got=got, turn=turns, gain=gain, here=w_here, there=w_there)
        if tick == 0:
            x, message, rows = step(got)
        else:
            there = (tick - 1) % 2
            pairs = [(s, there, s + 1, 1 - there) for s in range(sections - 1)]
            relayed = lax.ppermute(x, ALL, links(pairs))
            heard = lax.all_to_all(message, ALL, split_axis=0, concat_axis=0, axis_index_groups=relay_group(there), tiled=True)
            if tick == 1:
                tails = lax.ppermute(x, ALL, links([(sections - 1, 1, 0, 0), (1, 1, 0, 1)]))
            extra = got if tick == 1 else tails
            past = dict(spoken=messages, found=found) if tick == 3 else {}
            x, message, rows = step(relayed, heard=heard, extra=extra, **past)
        found = found + [rows]
        messages = messages + [message]

    told = lax.all_to_all(messages[3], RC, split_axis=0, concat_axis=0, tiled=True)
    swapped = lax.ppermute(rows, "row", [(0, 1), (1, 0)])
    out = finish(flags, rows, swapped, told, early, late)
    return out[None, :, None]


def solution(mesh):
    placed = (
        P("section", ("row", "col"), None),
        P(None, ("row", "col"), None),
        P("section", None),
        P("section", "row", "col"),
        P("section", None, ("row", "col"), None),
        P("section", None, ("row", "col"), None, None),
        P("section", None, ("row", "col"), None, None),
        P(None, ("row", "col")),
    )
    return jax.shard_map(
        inner,
        mesh=mesh,
        in_specs=placed,
        out_specs=P("section", None, ("row", "col"), None),
        check_vma=False,
    )
```

```python
import functools

import jax
import jax.numpy as jnp
import numpy as np
from jax import lax
from jax.experimental import pallas as pl
from jax.experimental.pallas import tpu as pltpu
from jax.sharding import PartitionSpec as P


QH = 64
KVH = 4
HD = 128
PER = QH // KVH
ALL = ("section", "row", "col")
RC = ("row", "col")
FACTOR = 1.0 / np.sqrt(HD)
bf16 = jnp.bfloat16
f32 = jnp.float32


def angles(positions):
    half = HD // 2
    steps_up = jnp.arange(half).astype(f32)
    inverse = jnp.exp(-jnp.log(f32(500000.0)) * steps_up / half)
    angle = positions.astype(f32)[:, None] * inverse[None, :]
    cosine = jnp.cos(angle)
    sine = jnp.sin(angle)
    return jnp.concatenate([cosine, cosine], 1), jnp.concatenate([-sine, sine], 1)


def attend(qs, k_ref, v_ref, lens, scores, ticks):
    for i, t in enumerate(ticks):
        for g in range(KVH):
            q = qs[t * QH + g * PER : t * QH + (g + 1) * PER, :].astype(bf16)
            k = k_ref[i, :, g * HD : (g + 1) * HD]
            scores[i * QH + g * PER : i * QH + (g + 1) * PER, :] = lax.dot_general(
                q, k, (((1,), (1,)), ((), ())), preferred_element_type=f32
            )
    means, lses = [], []
    lane = lax.broadcasted_iota(jnp.int32, (QH, HD), 1)
    for i, t in enumerate(ticks):
        part = scores[i * QH : (i + 1) * QH, :] * FACTOR
        part = jnp.where(lane < lens[t], part, f32(-1e30))
        top = jnp.max(part, axis=1, keepdims=True)
        weights = jnp.exp(part - top)
        total = jnp.sum(weights, axis=1, keepdims=True)
        probs = (weights / total).astype(bf16)
        lses.append(top + jnp.log(total))
        for g in range(KVH):
            v = v_ref[i, :, g * HD : (g + 1) * HD]
            means.append(jnp.dot(probs[g * PER : (g + 1) * PER], v, preferred_element_type=f32))
    return means, lses


def spread(lse, tick):
    hi = lse.astype(bf16).astype(f32)
    mid = (lse - hi).astype(bf16).astype(f32)
    low = (lse - hi) - mid
    lane = lax.broadcasted_iota(jnp.int32, (PER, HD), 1)
    row = lax.broadcasted_iota(jnp.int32, (PER, HD), 0)
    out = []
    for g in range(KVH):
        total = jnp.zeros((PER, HD), f32)
        for p, part in enumerate((hi, mid, low)):
            there = lane == row + (16 + 48 * (tick // 2) + 16 * p)
            total = total + jnp.where(there, part[g * PER : (g + 1) * PER], 0.0)
        out.append(jnp.sum(total, axis=0, keepdims=True))
    return out


def first_kernel(base, lengths, q_ref, k_ref, v_ref, mean_ref, fed_ref, aux_ref, qs, scores):
    lens = [lengths[base[0] + t] for t in range(4)]
    for h in range(QH):
        qs[pl.ds(h, 4, stride=QH), :] = q_ref[:, h * HD : (h + 1) * HD].astype(f32)
    means, lses = attend(qs, k_ref, v_ref, lens, scores, (0, 1, 2))
    for n, mean in enumerate(means):
        mean_ref[n * PER : (n + 1) * PER, :] = mean
        fed_ref[n * PER : (n + 1) * PER, :] = mean.astype(bf16)
    even, odd, late = (spread(lses[t], t) for t in (0, 1, 2))
    for g in range(KVH):
        aux_ref[g : g + 1, :] = even[g] + late[g]
        aux_ref[KVH + g : KVH + g + 1, :] = odd[g]


def second_kernel(base, lengths, pick, q_ref, k_ref, v_ref, row_ref, ent_ref, aux_in, mean_ref, own_ref, tail_ref, head_ref, ask_ref, aux_ref, qs, scores, wide, ents):
    blocks = 2 * QH
    lens = [lengths[base[0] + t] for t in range(4)]
    for h in range(QH):
        qs[pl.ds(h, 4, stride=QH), :] = q_ref[:, h * HD : (h + 1) * HD].astype(f32)
    for a in range(blocks):
        wide[a : a + 1, :] = row_ref[:, a * HD : (a + 1) * HD].astype(f32)
        ents[pl.ds(a, 3, stride=blocks), :] = ent_ref[:, a * HD : (a + 1) * HD].astype(f32)
    ask_ref[...] = qs[...].astype(bf16)
    own_ref[...] = wide[...].astype(bf16)
    chosen = pl.multiple_of(pick[0] * blocks + QH, QH)
    tail_ref[...] = ents[pl.ds(chosen, QH), :].astype(bf16)
    for t in range(3):
        head_ref[t * QH : (t + 1) * QH, :] = ents[t * blocks : t * blocks + QH, :].astype(bf16)
    means, lses = attend(qs, k_ref, v_ref, lens, scores, (3,))
    for n, mean in enumerate(means):
        mean_ref[n * PER : (n + 1) * PER, :] = mean
    late = spread(lses[0], 3)
    lane = lax.broadcasted_iota(jnp.int32, (1, HD), 1)
    for r in range(2):
        known = jnp.where(lane == 0, lens[r].astype(f32), 0.0)
        known = known + jnp.where(lane == 1, lens[2 + r].astype(f32), 0.0)
        for g in range(KVH):
            n = r * KVH + g
            row = aux_in[n : n + 1, :] + known
            aux_ref[n : n + 1, :] = row + late[g] if r else row


def third_kernel(flags, fed_ref, head_ref, own_ref, tail_ref, ask_ref, aux_ref, send_ref):
    first = jnp.full((3 * QH, HD), flags[0], jnp.int32) > 0
    fed = jnp.where(first, head_ref[...].astype(f32), fed_ref[...].astype(f32)).astype(bf16)
    own = own_ref[...]
    tail = tail_ref[...]
    pad = jnp.zeros((8, HD), f32)
    sub = lax.broadcasted_iota(jnp.int32, (8, HD), 0)
    for g in range(KVH):
        for r in range(2):
            aux = jnp.where(sub == 0, jnp.broadcast_to(aux_ref[r * KVH + g : r * KVH + g + 1, :], (8, HD)), pad)
            asks = [ask_ref[t * QH + g * PER : t * QH + (g + 1) * PER, :] for t in (r, 2 + r)]
            for c in (2 * g, 2 * g + 1):
                d = 8 * r + c
                if r == 0:
                    send_ref[d, : 2 * QH, :] = own
                    send_ref[d, 2 * QH : 3 * QH, :] = fed[QH : 2 * QH]
                else:
                    send_ref[d, :QH, :] = fed[2 * QH :]
                    send_ref[d, QH : 2 * QH, :] = tail
                    send_ref[d, 2 * QH : 3 * QH, :] = fed[:QH]
                send_ref[d, 3 * QH : 3 * QH + PER, :] = asks[0]
                send_ref[d, 3 * QH + PER : 3 * QH + 2 * PER, :] = asks[1]
                send_ref[d, 3 * QH + 2 * PER :, :] = aux.astype(bf16)


def prepare(queries, keys, values, row, entering, base, lengths, pick, first, shift):
    slots, kept = keys.shape[1], KVH * HD
    held = pl.BlockSpec(memory_space=pltpu.VMEM)
    small = pl.BlockSpec(memory_space=pltpu.SMEM)

    def cost(n):
        return pl.CostEstimate(flops=n, bytes_accessed=n, transcendentals=0)

    mean, fed, aux = pl.pallas_call(
        first_kernel,
        grid=(1,),
        out_shape=(
            jax.ShapeDtypeStruct((3 * QH, HD), f32),
            jax.ShapeDtypeStruct((3 * QH, HD), bf16),
            jax.ShapeDtypeStruct((2 * KVH, HD), f32),
        ),
        in_specs=[small, small, held, *[pl.BlockSpec((3, slots, kept), lambda i: (0, 0, 0))] * 2],
        out_specs=(held, held, held),
        scratch_shapes=[pltpu.VMEM((4 * QH, HD), f32), pltpu.VMEM((3 * QH, slots), f32)],
        cost_estimate=cost(4 << 20),
        name="first_part",
    )(base, lengths, queries, keys, values)
    fed = shift(fed)
    late, own, tail, head, ask, aux = pl.pallas_call(
        second_kernel,
        grid=(1,),
        out_shape=(
            jax.ShapeDtypeStruct((QH, HD), f32),
            jax.ShapeDtypeStruct((2 * QH, HD), bf16),
            jax.ShapeDtypeStruct((QH, HD), bf16),
            jax.ShapeDtypeStruct((3 * QH, HD), bf16),
            jax.ShapeDtypeStruct((4 * QH, HD), bf16),
            jax.ShapeDtypeStruct((2 * KVH, HD), f32),
        ),
        in_specs=[small, small, small, held, *[pl.BlockSpec((1, slots, kept), lambda i: (3, 0, 0))] * 2, held, held, held],
        out_specs=(held,) * 6,
        scratch_shapes=[
            pltpu.VMEM((4 * QH, HD), f32),
            pltpu.VMEM((QH, slots), f32),
            pltpu.VMEM((2 * QH, HD), f32),
            pltpu.VMEM((6 * QH, HD), f32),
        ],
        cost_estimate=cost(16 << 20),
        name="second_part",
    )(base, lengths, pick, queries, keys, values, row, entering, aux)
    sent = pl.pallas_call(
        third_kernel,
        out_shape=jax.ShapeDtypeStruct((16, 3 * QH + 2 * PER + 8, HD), bf16),
        in_specs=[small, held, held, held, held, held, held],
        out_specs=held,
        cost_estimate=cost(1 << 20),
        name="third_part",
    )(first, fed, head, own, tail, ask, aux)
    return sent, mean, late


def tick_kernel(tick, *refs):
    combined = tick > 0
    flags, a_ref, b_ref, ask_ref, aux_ref, turn_ref, gain_ref, here_ref, there_ref = refs[:9]
    refs = refs[9:]
    if combined:
        heard_ref, mean_ref, extra_ref = refs[:3]
        refs = refs[3:]
    if tick == 3:
        spoken, found, refs = refs[:3], refs[3:6], refs[6:]
        x_ref = None
        message_ref, pick_ref, scaled, exact, both = refs
    else:
        x_ref, message_ref, pick_ref, scaled, exact = refs
    half = QH * HD
    rows = a_ref.shape[0]
    first = jnp.full((rows, HD), flags[2], jnp.int32) > 0
    lane = lax.broadcasted_iota(jnp.int32, (rows, HD), 1)
    square = jnp.zeros((rows, HD), f32)
    for n in range(2 * QH):
        h = n % QH
        at = slice(h * HD, (h + 1) * HD)
        if n < QH:
            x = a_ref[:, at]
            if combined:
                if h % PER == 0:
                    g = h // PER
                    own = jnp.where(first, 0.0, heard_ref[2 * g].astype(f32))
                    new = heard_ref[2 * g + 1].astype(f32)
                mean = mean_ref[:, at].astype(f32)
                weight = own[:, h % PER : h % PER + 1]
                x = jnp.where(first, 0.0, x.astype(f32))
                x = (x + (mean + weight * (new - mean))).astype(bf16)
        else:
            x = b_ref[:, at]
            if combined:
                x = jnp.where(first, extra_ref[:, at].astype(f32), x.astype(f32)).astype(bf16)
        if tick < 3:
            x_ref[:, n * HD : (n + 1) * HD] = x
        wide = x.astype(f32)
        exact[n * rows : (n + 1) * rows, :] = wide
        square = square + wide * wide
        scaled[n // QH, :, at] = (wide * gain_ref[:, n * HD : (n + 1) * HD].astype(f32)).astype(bf16)
    fresh = jnp.zeros((rows, HD), f32)
    step = 2048
    for ref, part in ((here_ref, flags[0]), (there_ref, 1 - flags[0])):
        for k in range(0, half, step):
            fresh = fresh + jnp.dot(scaled[part, :, k : k + step], ref[k : k + step, :], preferred_element_type=f32)
    scale = lax.rsqrt(jnp.sum(square, axis=1, keepdims=True) / (2 * half) + 1e-05)
    fresh = fresh * scale
    k = tick // 2
    key = fresh * turn_ref[2 * k] + pltpu.roll(fresh, HD // 2, 1) * turn_ref[2 * k + 1]
    key = key.astype(bf16).astype(f32)
    score = jnp.zeros((rows, HD), f32)
    for i in range(PER):
        one = jnp.sum(ask_ref[:, i * HD : (i + 1) * HD].astype(f32) * key, axis=1, keepdims=True)
        score = jnp.where(lane == i, one, score)
    aux = aux_ref[:, :HD].astype(f32)
    lse = jnp.zeros((rows, HD), f32)
    for p in range(3):
        lse = lse + pltpu.roll(aux, HD - (16 + 48 * (tick // 2) + 16 * p), 1)
    own = jnp.where(lane < PER, 1.0 / (1.0 + jnp.exp(lse - score * FACTOR)), 0.0)
    is_key = jnp.full((rows, HD), flags[1], jnp.int32) > 0
    message = jnp.where(is_key, own, fresh).astype(bf16)
    even = jnp.full((2, HD), flags[0], jnp.int32) == 0
    for n in range(2 * QH):
        at = slice(n * HD, (n + 1) * HD)
        pair = exact[pl.ds(n * rows + flags[3], 2, stride=rows // 2), :]
        if tick == 3:
            early = jnp.where(even, found[0][:, at].astype(f32), found[1][:, at].astype(f32))
            late = jnp.where(even, found[2][:, at].astype(f32), pair)
            pair = jnp.concatenate([early, late], axis=0)
        pick_ref[:, at] = pair.astype(bf16)
    if tick < 3:
        for d in range(message_ref.shape[0]):
            message_ref[d] = message
        return
    even = jnp.full((rows, HD), flags[0], jnp.int32) == 0
    both[:rows, :] = jnp.where(even, spoken[0][0].astype(f32), spoken[1][0].astype(f32))
    both[rows:, :] = jnp.where(even, spoken[2][0].astype(f32), message.astype(f32))
    for j in range(rows):
        message_ref[j] = both[pl.ds(j, 2, stride=rows), :].astype(bf16)


def do_tick(tick, flags, x, got, turn, gain, here, there, heard=None, extra=None, spoken=(), found=()):
    rows, half = got.shape[0], QH * HD
    small = pl.BlockSpec(memory_space=pltpu.SMEM)
    held = pl.BlockSpec(memory_space=pltpu.VMEM)

    def block(size, n):
        return pl.BlockSpec((rows, size), lambda i: (0, n))

    k = tick // 2
    specs = [small, block(half, 0), block(half, 1), block(PER * HD, 12 + k), block(8 * HD, 28), held, held, held, held]
    operands = [flags, x, x, got, got, turn, gain, here, there]
    if tick:
        specs += [held, block(half, 0 if tick == 3 else 2), block(half, 1)]
        operands += [heard, got, extra]
    specs += [pl.BlockSpec((1, rows, HD), lambda i: (0, 0, 0))] * len(spoken)
    operands += spoken
    specs += [held] * len(found)
    operands += found
    return pl.pallas_call(
        functools.partial(tick_kernel, tick),
        grid=(1,),
        out_shape=(
            *[jax.ShapeDtypeStruct((rows, 2 * half), bf16)] * (tick < 3),
            jax.ShapeDtypeStruct((rows, 2 if tick == 3 else rows, HD), bf16),
            jax.ShapeDtypeStruct((4 if tick == 3 else 2, 2 * half), bf16),
        ),
        in_specs=specs,
        out_specs=(held,) * (3 if tick < 3 else 2),
        scratch_shapes=[
            pltpu.VMEM((2, rows, half), bf16),
            pltpu.VMEM((2 * QH * rows, HD), f32),
            *[pltpu.VMEM((2 * rows, HD), f32)] * (tick == 3),
        ],
        cost_estimate=pl.CostEstimate(flops=1 << 26, bytes_accessed=6 << 20, transcendentals=0),
        compiler_params=pltpu.CompilerParams(vmem_limit_bytes=20 << 20),
    )(*operands)


def last_kernel(flags, mine_ref, swap_ref, told_ref, early_ref, late_ref, out_ref, tell, mean):
    mean[: 3 * QH, :] = early_ref[...]
    mean[3 * QH :, :] = late_ref[...]
    for c in range(8):
        for r in range(2):
            for k in range(2):
                t = 2 * k + r
                tell[c, t : t + 1, :] = told_ref[8 * r + c, k : k + 1, :].astype(f32)
    even = jnp.full((4, HD), flags[0], jnp.int32) == 0
    for n in range(2 * QH):
        at = slice(n * HD, (n + 1) * HD)
        e = mine_ref[:, at].astype(f32)
        f = swap_ref[:, at].astype(f32)
        a = jnp.concatenate([e[0:1], f[0:1], e[2:3], f[2:3]], axis=0)
        b = jnp.concatenate([f[1:2], e[1:2], f[3:4], e[3:4]], axis=0)
        x = jnp.where(even, a, b)
        if n < QH:
            g, i = n // PER, n % PER
            cached = mean[pl.ds(n, 4, stride=QH), :]
            own = tell[2 * g][:, i : i + 1]
            x = x + (cached + own * (tell[2 * g + 1] - cached))
        out_ref[:, at] = x.astype(bf16)


def finish(flags, mine, swapped, told, early, late):
    held = pl.BlockSpec(memory_space=pltpu.VMEM)
    return pl.pallas_call(
        last_kernel,
        out_shape=jax.ShapeDtypeStruct((4, mine.shape[1]), bf16),
        in_specs=[pl.BlockSpec(memory_space=pltpu.SMEM), *[held] * 5],
        out_specs=held,
        scratch_shapes=[pltpu.VMEM((8, 4, HD), f32), pltpu.VMEM((4 * QH, HD), f32)],
        cost_estimate=pl.CostEstimate(flops=1 << 20, bytes_accessed=1 << 20, transcendentals=0),
        compiler_params=pltpu.CompilerParams(vmem_limit_bytes=8 << 20),
        name="last_part",
    )(flags, mine, swapped, told, early, late)


def inner(arriving, entering, gain, kv_weight, queries, cache_keys, cache_values, lengths):
    section_at = lax.axis_index("section")
    row_at = lax.axis_index("row")
    col_at = lax.axis_index("col")
    sections = lax.axis_size("section")
    cols = lax.axis_size("col")
    ticks = queries.shape[1]
    width = arriving.shape[2]
    half = width // 2
    last = section_at == sections - 1
    first = section_at == 0

    def at(s, r, c):
        return ((s % sections) * 2 + r) * cols + c

    def links(pairs):
        return [(at(s, r, c), at(v, w, c)) for s, r, v, w in pairs for c in range(cols)]

    def relay_group(r):
        return [
            [at(s, r, c) for c in range(cols)] + [at(s + 1, 1 - r, c) for c in range(cols)]
            for s in range(sections)
        ]

    w_here = kv_weight[0]
    w_there = lax.ppermute(w_here, "row", [(0, 1), (1, 0)])
    pick = jnp.where(first, 0, jnp.where(last, 1, 2)).astype(jnp.int32)[None]
    sent, early, late = prepare(
        queries[0, :, 0],
        cache_keys[0, :, 0],
        cache_values[0, :, 0],
        arriving[0],
        entering[:, 0],
        (sections - 1 - section_at).astype(jnp.int32)[None],
        lengths[:, 0],
        pick,
        first.astype(jnp.int32)[None],
        lambda fed: lax.ppermute(fed, "section", [(s, s + 1) for s in range(sections - 1)]),
    )
    got = lax.all_to_all(sent, RC, split_axis=0, concat_axis=0, tiled=True)
    got = got.reshape(2 * cols, -1)

    aux_at = width + half + 2 * PER * HD
    turns = jnp.stack([t for k in range(2) for t in angles(got[:, aux_at + k].astype(f32))])
    flags = jnp.stack([row_at, 1 - col_at % 2, first.astype(jnp.int32), col_at]).astype(jnp.int32)

    found, messages = [], []
    for tick in range(ticks):
        step = functools.partial(do_tick, tick, flags, got=got, turn=turns, gain=gain, here=w_here, there=w_there)
        if tick == 0:
            x, message, rows = step(got)
        else:
            there = (tick - 1) % 2
            pairs = [(s, there, s + 1, 1 - there) for s in range(sections - 1)]
            relayed = lax.ppermute(x, ALL, links(pairs))
            heard = lax.all_to_all(message, ALL, split_axis=0, concat_axis=0, axis_index_groups=relay_group(there), tiled=True)
            if tick == 1:
                tails = lax.ppermute(x, ALL, links([(sections - 1, 1, 0, 0), (1, 1, 0, 1)]))
            extra = got if tick == 1 else tails
            past = dict(spoken=messages, found=found) if tick == 3 else {}
            *x, message, rows = step(relayed, heard=heard, extra=extra, **past)
            x = x[0] if x else None
        found = found + [rows]
        messages = messages + [message]

    told = lax.all_to_all(messages[3], RC, split_axis=0, concat_axis=0, tiled=True)
    swapped = lax.ppermute(rows, "row", [(0, 1), (1, 0)])
    out = finish(flags, rows, swapped, told, early, late)
    return out[None, :, None]


def solution(mesh):
    placed = (
        P("section", ("row", "col"), None),
        P(None, ("row", "col"), None),
        P("section", None),
        P("section", "row", "col"),
        P("section", None, ("row", "col"), None),
        P("section", None, ("row", "col"), None, None),
        P("section", None, ("row", "col"), None, None),
        P(None, ("row", "col")),
    )
    return jax.shard_map(
        inner,
        mesh=mesh,
        in_specs=placed,
        out_specs=P("section", None, ("row", "col"), None),
        check_vma=False,
    )
```
